512 devices in a mesh: row: 32 (over y, z_lo), col: 16 (over z_hi, x, core).
Axes of the slice: x: 4, y: 8, z: 8 (z_hi: 2, z_lo: 4; z = z_hi * 4 + z_lo), core: 2. Of those that a mesh axis runs over, the one named last changes fastest.
Arguments:
- embeddings: bfloat16 [8192, 256], P(('row', 'col')), may hold values from -6 to 6
- labels: bfloat16 [8192, 1024], P(('row', 'col')), may hold values from -6 to 6
- tile_mask: int32 [32, 32], replicated, may hold values 0 or 1
Outputs:
- spread_labels: bfloat16 [8192, 1024], P(('row', 'col'))
The draws below stay inside these ranges and needn't reach their ends.
Inputs may be any that keep to these rules, and one draw needn't show every extreme that they name: Only the entries tile_mask[i, j] with i < j are read; the tile of blocks i and j (and of j and i) is kept where it is 1.
All inputs are finite; a program needn't handle non-finite values.
Results may differ from the reference program's by a relative error of at most 0.015.
Values may be sent and summed in bfloat16 or wider, within the bound.
A program may use at most 64 MiB of HBM per device.

```python
import math
import jax
import jax.numpy as jnp
from jax import lax

E = 256
C = 1024
BLOCK = 256
ITERS = 2
IMAGES = 8192
BLOCKS = 32


def place_ends(array, own_key, smallest, high):
    longest = array.shape.index(max(array.shape))
    spots = []
    for shift in (0, 1):
        where = [jax.random.randint(jax.random.fold_in(own_key, axis), (), 0, length) for axis, length in enumerate(array.shape)]
        where[longest] = (where[longest] + shift) % array.shape[longest]
        spots.append(tuple(where))
    return array.at[spots[0]].set(smallest).at[spots[1]].set(high)


def level_of(rng, dims, shards, low, high):
    loudness = 1.0
    for position, shards_of in shards:
        heights = jax.random.uniform(jax.random.fold_in(jax.random.fold_in(rng, 6), position), (shards_of,), jnp.float32, low / len(shards), high / len(shards))
        loudness = loudness * jnp.repeat(jnp.exp(heights), dims[position] // shards_of).reshape((-1,) + (1,) * (len(dims) - 1 - position))
    return loudness


def noise(rng, dims, scale, limit, split=(), held_as=jnp.bfloat16):
    values = jax.random.normal(rng, dims, jnp.float32) * scale
    if len(split) > 0:
        values = level_of(rng, dims, split, -0.22, 0.18) * values
    return jnp.clip(values, min=-limit, max=limit).astype(held_as)


def setup_inputs(seed: int = 0) -> dict:
    streams_of = jax.random.split(jax.random.key(seed), 4)
    return {
        "embeddings": noise(streams_of[0], (IMAGES, E), 1.0, 6.0, ((0, 512),)),
        "labels": noise(streams_of[1], (IMAGES, C), 1.0, 6.0, ((0, 512),)),
        "tile_mask": place_ends((jax.random.randint(streams_of[2], (BLOCKS, BLOCKS), 0, 4) < 3).astype(jnp.int32), jax.random.fold_in(streams_of[2], 1), 0, 1),
    }


MIXING = 0.9
SHARPNESS = 3.0
EPSILON = 1e-06

def unit_rows(embeddings):
    values = embeddings.astype(jnp.float32)
    return (values * lax.rsqrt(lax.optimization_barrier(jnp.sum(values * values, axis=1, keepdims=True)) + EPSILON)).astype(jnp.bfloat16)

def symmetric_keep(tile_mask):
    blocks = tile_mask.shape[0]
    block_row = lax.broadcasted_iota(jnp.int32, (blocks, blocks), 0)
    block_col = lax.broadcasted_iota(jnp.int32, (blocks, blocks), 1)
    mirrored = jnp.where(block_row < block_col, tile_mask, tile_mask.T)
    return jnp.where(block_row == block_col, 1, mirrored)

def reference(embeddings, labels, tile_mask):
    unit_vecs = unit_rows(embeddings)
    kept_sym = symmetric_keep(tile_mask).astype(jnp.float32)
    sharpness = SHARPNESS * math.sqrt(E)
    all_ids = jnp.arange(IMAGES, dtype=jnp.int32)
    block_list = jnp.arange(BLOCKS, dtype=jnp.int32)

    def kernel_block(block_index):
        offset_rows = (block_index * BLOCK).astype(jnp.int32)
        block_vecs = lax.dynamic_slice_in_dim(unit_vecs, offset_rows, BLOCK, 0)
        cosine = jnp.dot(block_vecs, unit_vecs.T, preferred_element_type=jnp.float32)
        kept_row = jnp.repeat(kept_sym[block_index], BLOCK)
        own_ids = offset_rows + jnp.arange(BLOCK, dtype=jnp.int32)
        distinct = own_ids[:, None] != all_ids[None, :]
        return jnp.where(distinct, jnp.exp(sharpness * cosine) * kept_row[None, :], jnp.zeros_like(cosine)).astype(jnp.bfloat16)
    degree = lax.map(lambda index: lax.optimization_barrier(jnp.sum(kernel_block(index), axis=1, dtype=jnp.float32)), block_list).reshape(IMAGES)
    inv_root = lax.rsqrt(degree)
    seed_scores = labels.astype(jnp.float32)
    current = seed_scores
    for iteration in range(ITERS):
        scaled = (inv_root[:, None] * current).astype(jnp.bfloat16)
        spread = lax.map(lambda index: jnp.dot(kernel_block(index), scaled, preferred_element_type=jnp.float32), block_list).reshape(IMAGES, C)
        current = MIXING * inv_root[:, None] * spread + (1.0 - MIXING) * seed_scores
    return current.astype(jnp.bfloat16)
```

```python
import math

import jax
import jax.numpy as jnp
from jax import lax
from jax.experimental import pallas as pl
from jax.experimental.pallas import tpu as pltpu
from jax.sharding import PartitionSpec as P

MIXING = 0.9
SHARPNESS = 3.0
EPSILON = 1e-06

SIDE = 8
CHUNK = 128
PIECE = 16
LANES = 128
MESH = pl.DeviceIdType.MESH
FAR_FIRST = (4, 3, 5, 2, 6, 1, 7)
NEAR_FIRST = (1, 7, 2, 6, 3, 5, 4)

UNIT_SWAP, LABEL_SWAP, UNIT_GATHER, UNIT_PASS, LABEL_GATHER, DEGREE, REDUCE1, GATHER2, REDUCE2, FINAL = range(10)
PHASES = 10


def spread_kernel(
    mask_ref,
    emb_ref,
    lab_ref,
    out_ref,
    uj,
    ui,
    kmat,
    lab,
    sc1,
    sc2,
    part1,
    part2,
    rcv1,
    rcv2,
    deg,
    fin,
    outb,
    send_sem,
    recv_sem,
):
    row = lax.axis_index("row")
    col = lax.axis_index("col")
    y = lax.div(row, 4)
    z_lo = lax.rem(row, 4)
    z_hi = lax.div(col, 8)
    c = lax.rem(col, 8)
    core = lax.rem(col, 2)
    z = z_hi * 4 + z_lo

    def at(new_y, new_z):
        return (new_y * 4 + lax.rem(new_z, 4), lax.div(new_z, 4) * 8 + c)

    def gather_peer(k):
        return at(lax.rem(y + core * k, SIDE), lax.rem(z + (1 - core) * k, SIDE))

    def reduce_peer(k):
        return at(lax.rem(y + (1 - core) * k, SIDE), lax.rem(z + core * k, SIDE))

    def swap_index(k):
        return lax.rem(c + k, SIDE)

    def swap_peer(k):
        return (row, z_hi * 8 + swap_index(k))

    partner = (row, z_hi * 8 + (c + 1 - 2 * core))

    barrier = pltpu.get_barrier_semaphore()
    for k in range(1, SIDE):
        for peer in (gather_peer(k), reduce_peer(k), swap_peer(k)):
            pl.semaphore_signal(barrier, inc=1, device_id=peer, device_id_type=MESH)

    started = []

    def send(phase, k, src, dst, device):
        copy = pltpu.make_async_remote_copy(
            src_ref=src,
            dst_ref=dst,
            send_sem=send_sem.at[phase, k],
            recv_sem=recv_sem.at[phase, k],
            device_id=device,
            device_id_type=MESH,
        )
        copy.start()
        started.append(copy)
        return copy

    own_rows = pl.ds(pl.multiple_of(c * PIECE, PIECE), PIECE)
    own_lanes = pl.ds(pl.multiple_of(c * LANES, LANES), LANES)
    values = emb_ref[...].astype(jnp.float32)
    norm = lax.rsqrt(jnp.sum(values * values, axis=1, keepdims=True) + EPSILON)
    uj[0, own_rows, :] = (values * norm).astype(jnp.bfloat16)
    lab[0, own_rows, :] = lab_ref[:, own_lanes]

    pl.semaphore_wait(barrier, 3 * (SIDE - 1))

    unit_swaps = [
        send(UNIT_SWAP, k, uj.at[0, own_rows, :], uj.at[0, own_rows, :], swap_peer(k)) for k in range(1, SIDE)
    ]
    label_swaps = []
    for k in range(1, SIDE):
        lanes = pl.ds(pl.multiple_of(swap_index(k) * LANES, LANES), LANES)
        label_swaps.append(
            send(LABEL_SWAP, k, lab_ref.at[:, lanes], lab.at[0, own_rows, :], swap_peer(k))
        )

    for copy in unit_swaps:
        copy.wait_recv()
    unit_gathers = {
        k: send(UNIT_GATHER, k, uj.at[0], uj.at[k], gather_peer(k)) for k in FAR_FIRST
    }
    for copy in label_swaps:
        copy.wait_recv()
    label_gathers = [
        send(LABEL_GATHER, k, lab.at[0], lab.at[k], gather_peer(k)) for k in FAR_FIRST
    ]
    ui[0] = uj[0]
    unit_passes = []
    for k in NEAR_FIRST:
        unit_gathers[k].wait_recv()
        unit_passes.append(send(UNIT_PASS, k, uj.at[k], ui.at[k], partner))
    for copy in unit_passes:
        copy.wait_recv()

    scale = SHARPNESS * math.sqrt(emb_ref.shape[1]) * math.log2(math.e)
    lane = lax.broadcasted_iota(jnp.int32, (1, 2 * CHUNK), 1)

    def block_of(chunk_y, chunk_z):
        return chunk_y * 4 + lax.rem(chunk_z, 4)

    def back(position, k):
        return lax.rem(position + SIDE - k, SIDE)

    def kept(row_block, col_block):
        low = jnp.minimum(row_block, col_block)
        high = jnp.maximum(row_block, col_block)
        return jnp.where(row_block == col_block, 1, mask_ref[low, high]).astype(jnp.float32)

    def make_columns(group, carry):
        columns = uj[pl.ds(2 * group, 2)].reshape(2 * CHUNK, emb_ref.shape[1])
        col_blocks = [
            block_of(back(y, core * (2 * group + half)), back(z, (1 - core) * (2 * group + half)))
            for half in range(2)
        ]
        sums = jnp.zeros((1, 2 * CHUNK), jnp.float32)
        for k in range(SIDE):
            row_block = block_of(back(y, (1 - core) * k), back(z, core * k))
            cosine = lax.dot_general(
                ui[k], columns, (((1,), (1,)), ((), ())), preferred_element_type=jnp.float32
            )
            keep = jnp.where(
                lane < CHUNK, kept(row_block, col_blocks[0]), kept(row_block, col_blocks[1])
            )
            weights = jnp.exp2(cosine * scale) * keep
            if k == 0:
                own_row = lax.broadcasted_iota(jnp.int32, weights.shape, 0)
                own_col = lax.broadcasted_iota(jnp.int32, weights.shape, 1) + group * (2 * CHUNK)
                weights = jnp.where(own_row == own_col, 0.0, weights)
            weights = weights.astype(jnp.bfloat16)
            kmat[group, k * CHUNK : (k + 1) * CHUNK, :] = weights
            sums = sums + jnp.sum(weights.astype(jnp.float32), axis=0, keepdims=True)
        deg[0, pl.ds(2 * group, 1), :] = sums[:, :CHUNK]
        deg[0, pl.ds(2 * group + 1, 1), :] = sums[:, CHUNK:]
        return carry

    lax.fori_loop(0, SIDE // 2, make_columns, 0)

    degrees = [send(DEGREE, k, deg.at[0], deg.at[k], gather_peer(k)) for k in FAR_FIRST]
    for copy in label_gathers:
        copy.wait_recv()
    for copy in degrees:
        copy.wait_recv()
    degree = deg[0]
    for k in range(1, SIDE):
        degree = degree + pltpu.roll(deg[k], k, 0)
    inv_root = jnp.transpose(lax.rsqrt(degree))
    for k in range(SIDE):
        sc1[k] = (lab[k].astype(jnp.float32) * inv_root[:, k : k + 1]).astype(jnp.bfloat16)
    own_root = inv_root[:, 0:1]
    seeds = lab[0].astype(jnp.float32)

    def spread_rows(scaled, k):
        total = jnp.zeros((CHUNK, LANES), jnp.float32)
        for group in range(SIDE // 2):
            total = total + jnp.dot(
                kmat[group, k * CHUNK : (k + 1) * CHUNK, :],
                scaled[2 * group : 2 * group + 2].reshape(2 * CHUNK, LANES),
                preferred_element_type=jnp.float32,
            )
        return total

    def iterate(phase, scaled, part, rcv):
        copies = []
        for k in FAR_FIRST:
            part[k] = spread_rows(scaled, k).astype(jnp.bfloat16)
            copies.append(send(phase, k, part.at[k], rcv.at[k], reduce_peer(SIDE - k)))
        spread = spread_rows(scaled, 0)
        for copy in copies:
            copy.wait_recv()
        for k in range(1, SIDE):
            spread = spread + rcv[k].astype(jnp.float32)
        return MIXING * own_root * spread + (1.0 - MIXING) * seeds

    current = iterate(REDUCE1, sc1, part1, rcv1)
    sc2[0] = (own_root * current).astype(jnp.bfloat16)
    gathers = [send(GATHER2, k, sc2.at[0], sc2.at[k], gather_peer(k)) for k in FAR_FIRST]
    for copy in gathers:
        copy.wait_recv()
    current = iterate(REDUCE2, sc2, part2, rcv2)
    fin[...] = current.astype(jnp.bfloat16)
    outb[:, own_lanes] = fin[own_rows, :]
    finals = []
    for k in range(1, SIDE):
        rows = pl.ds(pl.multiple_of(swap_index(k) * PIECE, PIECE), PIECE)
        finals.append(send(FINAL, k, fin.at[rows, :], outb.at[:, own_lanes], swap_peer(k)))
    for copy in finals:
        copy.wait_recv()
    out_ref[...] = outb[...]
    for copy in started:
        copy.wait_send()


def shards(embeddings, labels, tile_mask):
    width = embeddings.shape[1]
    vmem = pl.BlockSpec(memory_space=pltpu.VMEM)
    chunks = (SIDE, CHUNK, LANES)
    return pl.pallas_call(
        spread_kernel,
        out_shape=jax.ShapeDtypeStruct(labels.shape, jnp.bfloat16),
        in_specs=[pl.BlockSpec(memory_space=pltpu.SMEM), vmem, vmem],
        out_specs=vmem,
        scratch_shapes=[
            pltpu.VMEM((SIDE, CHUNK, width), jnp.bfloat16),
            pltpu.VMEM((SIDE, CHUNK, width), jnp.bfloat16),
            pltpu.VMEM((SIDE // 2, SIDE * CHUNK, 2 * CHUNK), jnp.bfloat16),
            pltpu.VMEM(chunks, jnp.bfloat16),
            pltpu.VMEM(chunks, jnp.bfloat16),
            pltpu.VMEM(chunks, jnp.bfloat16),
            pltpu.VMEM(chunks, jnp.bfloat16),
            pltpu.VMEM(chunks, jnp.bfloat16),
            pltpu.VMEM(chunks, jnp.bfloat16),
            pltpu.VMEM(chunks, jnp.bfloat16),
            pltpu.VMEM((SIDE, SIDE, CHUNK), jnp.float32),
            pltpu.VMEM((CHUNK, LANES), jnp.bfloat16),
            pltpu.VMEM(labels.shape, jnp.bfloat16),
            pltpu.SemaphoreType.DMA((PHASES, SIDE)),
            pltpu.SemaphoreType.DMA((PHASES, SIDE)),
        ],
        compiler_params=pltpu.CompilerParams(collective_id=0, has_side_effects=True),
    )(tile_mask, embeddings, labels)


def solution(mesh):
    placed = (P(("row", "col"), None), P(("row", "col"), None), P())
    return jax.shard_map(
        shards, mesh=mesh, in_specs=placed, out_specs=P(("row", "col"), None), check_vma=False
    )
```

```python
import math

import jax
import jax.numpy as jnp
from jax import lax
from jax.experimental import pallas as pl
from jax.experimental.pallas import tpu as pltpu
from jax.sharding import PartitionSpec as P

MIXING = 0.9
SHARPNESS = 3.0
EPSILON = 1e-06

SIDE = 8
CHUNK = 128
PIECE = 16
LANES = 128
MESH = pl.DeviceIdType.MESH
FAR_FIRST = (4, 3, 5, 2, 6, 1, 7)
NEAR_FIRST = (1, 7, 2, 6, 3, 5, 4)

HALF = CHUNK // 2
UNIT_SWAP, LABEL_SWAP, UNIT_GATHER, UNIT_PASS, LABEL_GATHER, DEGREE = range(6)
REDUCE1, GATHER2, REDUCE2 = (6, 7), (8, 9), (10, 11)
FINAL = 12
PHASES = 13
LOAD_UNITS, LOAD_LABELS, LOAD_MASK, STORE_OWN = range(4)


def spread_kernel(
    mask_hbm,
    emb_hbm,
    lab_hbm,
    out_hbm,
    mask_ref,
    emb_ref,
    uj,
    ui,
    kmat,
    lab,
    sc1,
    sc2,
    part1,
    part2,
    rcv1,
    rcv2,
    deg,
    fin,
    send_sem,
    recv_sem,
    local_sem,
):
    row = lax.axis_index("row")
    col = lax.axis_index("col")
    y = lax.div(row, 4)
    z_lo = lax.rem(row, 4)
    z_hi = lax.div(col, 8)
    c = lax.rem(col, 8)
    core = lax.rem(col, 2)
    z = z_hi * 4 + z_lo

    def at(new_y, new_z):
        return (new_y * 4 + lax.rem(new_z, 4), lax.div(new_z, 4) * 8 + c)

    def gather_peer(k):
        return at(lax.rem(y + core * k, SIDE), lax.rem(z + (1 - core) * k, SIDE))

    def reduce_peer(k):
        return at(lax.rem(y + (1 - core) * k, SIDE), lax.rem(z + core * k, SIDE))

    def swap_index(k):
        return lax.rem(c + k, SIDE)

    def swap_peer(k):
        return (row, z_hi * 8 + swap_index(k))

    partner = (row, z_hi * 8 + (c + 1 - 2 * core))

    own_rows = pl.ds(pl.multiple_of(c * PIECE, PIECE), PIECE)
    own_lanes = pl.ds(pl.multiple_of(c * LANES, LANES), LANES)

    def local(slot, src, dst):
        copy = pltpu.make_async_copy(src, dst, local_sem.at[slot])
        copy.start()
        return copy

    load_units = local(LOAD_UNITS, emb_hbm, emb_ref)
    load_labels = local(LOAD_LABELS, lab_hbm.at[:, own_lanes], lab.at[0, own_rows, :])
    load_mask = local(LOAD_MASK, mask_hbm, mask_ref)
    barrier = pltpu.get_barrier_semaphore()
    for k in range(1, SIDE):
        for peer in (gather_peer(k), reduce_peer(k), swap_peer(k)):
            pl.semaphore_signal(barrier, inc=1, device_id=peer, device_id_type=MESH)

    def describe(phase, src, dst, device, slot=None):
        return pltpu.make_async_remote_copy(
            src_ref=src,
            dst_ref=dst,
            send_sem=send_sem.at[phase],
            recv_sem=recv_sem.at[phase if slot is None else PHASES + slot],
            device_id=device,
            device_id_type=MESH,
        )

    def send(phase, src, dst, device, slot=None):
        copy = describe(phase, src, dst, device, slot)
        copy.start()
        return copy

    sent = []

    def whole(phase, ref):
        copy = describe(phase, ref, ref, partner)
        sent.append(copy)
        return copy

    load_units.wait()
    values = emb_ref[...].astype(jnp.float32)
    norm = lax.rsqrt(jnp.sum(values * values, axis=1, keepdims=True) + EPSILON)
    uj[0, own_rows, :] = (values * norm).astype(jnp.bfloat16)

    pl.semaphore_wait(barrier, 3 * (SIDE - 1))

    for k in range(1, SIDE):
        send(UNIT_SWAP, uj.at[0, own_rows, :], uj.at[0, own_rows, :], swap_peer(k))
    for k in range(1, SIDE):
        lanes = pl.ds(pl.multiple_of(swap_index(k) * LANES, LANES), LANES)
        send(LABEL_SWAP, lab_hbm.at[:, lanes], lab.at[0, own_rows, :], swap_peer(k))

    others = slice(1, SIDE)
    whole(UNIT_SWAP, uj.at[0, 0 : (SIDE - 1) * PIECE, :]).wait_recv()
    unit_gathers = {
        k: send(UNIT_GATHER, uj.at[0], uj.at[k], gather_peer(k), slot=k - 1) for k in FAR_FIRST
    }
    whole(UNIT_GATHER, uj.at[others])
    load_labels.wait()
    whole(LABEL_SWAP, lab.at[0, 0 : (SIDE - 1) * PIECE, :]).wait_recv()
    for k in FAR_FIRST:
        send(LABEL_GATHER, lab.at[0], lab.at[k], gather_peer(k))
    ui[0] = uj[0]
    for k in NEAR_FIRST:
        unit_gathers[k].wait_recv()
        send(UNIT_PASS, uj.at[k], ui.at[k], partner)
    whole(UNIT_PASS, ui.at[others]).wait_recv()
    load_mask.wait()

    scale = SHARPNESS * math.sqrt(emb_ref.shape[1]) * math.log2(math.e)
    lane = lax.broadcasted_iota(jnp.int32, (1, 2 * CHUNK), 1)

    def block_of(chunk_y, chunk_z):
        return chunk_y * 4 + lax.rem(chunk_z, 4)

    def back(position, k):
        return lax.rem(position + SIDE - k, SIDE)

    def kept(row_block, col_block):
        low = jnp.minimum(row_block, col_block)
        high = jnp.maximum(row_block, col_block)
        return jnp.where(row_block == col_block, 1, mask_ref[low, high]).astype(jnp.float32)

    def make_columns(group, carry):
        columns = uj[pl.ds(2 * group, 2)].reshape(2 * CHUNK, emb_ref.shape[1])
        col_blocks = [
            block_of(back(y, core * (2 * group + half)), back(z, (1 - core) * (2 * group + half)))
            for half in range(2)
        ]
        sums = jnp.zeros((1, 2 * CHUNK), jnp.float32)
        for k in range(SIDE):
            row_block = block_of(back(y, (1 - core) * k), back(z, core * k))
            cosine = lax.dot_general(
                ui[k], columns, (((1,), (1,)), ((), ())), preferred_element_type=jnp.float32
            )
            keep = jnp.where(
                lane < CHUNK, kept(row_block, col_blocks[0]), kept(row_block, col_blocks[1])
            )
            weights = jnp.exp2(cosine * scale) * keep
            if k == 0:
                own_row = lax.broadcasted_iota(jnp.int32, weights.shape, 0)
                own_col = lax.broadcasted_iota(jnp.int32, weights.shape, 1) + group * (2 * CHUNK)
                weights = jnp.where(own_row == own_col, 0.0, weights)
            weights = weights.astype(jnp.bfloat16)
            kmat[k, :, pl.ds(pl.multiple_of(group * 2 * CHUNK, 2 * CHUNK), 2 * CHUNK)] = weights
            sums = sums + jnp.sum(weights.astype(jnp.float32), axis=0, keepdims=True)
        deg[0, pl.ds(2 * group, 1), :] = sums[:, :CHUNK]
        deg[0, pl.ds(2 * group + 1, 1), :] = sums[:, CHUNK:]
        return carry

    lax.fori_loop(0, SIDE // 2, make_columns, 0)

    for k in FAR_FIRST:
        send(DEGREE, deg.at[0], deg.at[k], gather_peer(k))
    whole(LABEL_GATHER, lab.at[others]).wait_recv()
    whole(DEGREE, deg.at[others]).wait_recv()
    degree = deg[0]
    for k in range(1, SIDE):
        degree = degree + pltpu.roll(deg[k], k, 0)
    inv_root = jnp.transpose(lax.rsqrt(degree))
    for k in range(SIDE):
        sc1[k] = (lab[k].astype(jnp.float32) * inv_root[:, k : k + 1]).astype(jnp.bfloat16)
    own_root = inv_root[:, 0:1]
    seeds = lab[0].astype(jnp.float32)

    def rows_of(half):
        return pl.ds(half * HALF, HALF)

    def iterate(phases, scaled, part, rcv, finish):
        spreads = []
        for half in range(2):
            rows = rows_of(half)
            spread = jnp.dot(
                kmat[:, rows, :].reshape(SIDE * HALF, SIDE * CHUNK),
                scaled[...].reshape(SIDE * CHUNK, LANES),
                preferred_element_type=jnp.float32,
            ).reshape(SIDE, HALF, LANES)
            spreads.append(spread[0])
            for k in FAR_FIRST:
                part[k, rows, :] = spread[k].astype(jnp.bfloat16)
            for k in FAR_FIRST:
                send(phases[half], part.at[k, rows, :], rcv.at[k, rows, :], reduce_peer(SIDE - k))
        for half in range(2):
            whole(phases[half], rcv.at[others, rows_of(half), :]).wait_recv()
            total = spreads[half]
            for k in range(1, SIDE):
                total = total + rcv[k, rows_of(half), :].astype(jnp.float32)
            rows = slice(half * HALF, (half + 1) * HALF)
            finish(half, MIXING * own_root[rows] * total + (1.0 - MIXING) * seeds[rows])

    def finish_first(half, current):
        rows = rows_of(half)
        root = own_root[half * HALF : (half + 1) * HALF]
        sc2[0, rows, :] = (root * current).astype(jnp.bfloat16)
        for k in FAR_FIRST:
            send(GATHER2[half], sc2.at[0, rows, :], sc2.at[k, rows, :], gather_peer(k))

    def finish_last(half, current):
        fin[rows_of(half), :] = current.astype(jnp.bfloat16)

    iterate(REDUCE1, sc1, part1, rcv1, finish_first)
    for half in range(2):
        whole(GATHER2[half], sc2.at[others, rows_of(half), :]).wait_recv()
    iterate(REDUCE2, sc2, part2, rcv2, finish_last)
    store_own = local(STORE_OWN, fin.at[own_rows, :], out_hbm.at[:, own_lanes])
    for k in range(1, SIDE):
        rows = pl.ds(pl.multiple_of(swap_index(k) * PIECE, PIECE), PIECE)
        send(FINAL, fin.at[rows, :], out_hbm.at[:, own_lanes], swap_peer(k))
    whole(FINAL, fin.at[0 : (SIDE - 1) * PIECE, :]).wait_recv()
    store_own.wait()
    for copy in sent:
        copy.wait_send()


def shards(embeddings, labels, tile_mask):
    width = embeddings.shape[1]
    anywhere = pl.BlockSpec(memory_space=pl.ANY)
    units = pltpu.VMEM((SIDE, CHUNK, width), jnp.bfloat16)
    chunks = pltpu.VMEM((SIDE, CHUNK, LANES), jnp.bfloat16)
    return pl.pallas_call(
        spread_kernel,
        out_shape=jax.ShapeDtypeStruct(labels.shape, jnp.bfloat16),
        in_specs=[anywhere] * 3,
        out_specs=anywhere,
        scratch_shapes=[
            pltpu.SMEM(tile_mask.shape, jnp.int32),
            pltpu.VMEM(embeddings.shape, jnp.bfloat16),
            units,
            units,
            pltpu.VMEM((SIDE, CHUNK, SIDE * CHUNK), jnp.bfloat16),
            chunks,
            chunks,
            chunks,
            chunks,
            chunks,
            chunks,
            chunks,
            pltpu.VMEM((SIDE, SIDE, CHUNK), jnp.float32),
            pltpu.VMEM((CHUNK, LANES), jnp.bfloat16),
            pltpu.SemaphoreType.DMA((PHASES,)),
            pltpu.SemaphoreType.DMA((PHASES + SIDE - 1,)),
            pltpu.SemaphoreType.DMA((4,)),
        ],
        compiler_params=pltpu.CompilerParams(collective_id=0, has_side_effects=True),
    )(tile_mask, embeddings, labels)


def solution(mesh):
    placed = (P(("row", "col"), None), P(("row", "col"), None), P())
    return jax.shard_map(
        shards, mesh=mesh, in_specs=placed, out_specs=P(("row", "col"), None), check_vma=False
    )
```

```python
import math

import jax
import jax.numpy as jnp
from jax import lax
from jax.experimental import pallas as pl
from jax.experimental.pallas import tpu as pltpu
from jax.sharding import PartitionSpec as P

MIXING = 0.9
SHARPNESS = 3.0
EPSILON = 1e-06

SIDE = 8
CHUNK = 128
PIECE = 16
LANES = 128
MESH = pl.DeviceIdType.MESH
FAR_FIRST = (4, 3, 5, 2, 6, 1, 7)
NEAR_FIRST = (1, 7, 2, 6, 3, 5, 4)

HALF = CHUNK // 2
UNIT_SWAP, LABEL_SWAP, UNIT_GATHER, UNIT_PASS, LABEL_GATHER, DEGREE = range(6)
REDUCE1, GATHER2, REDUCE2 = (6, 7), (8, 9), (10, 11)
FINAL, PIECE_GATHER, CROSS = 12, 13, 14
PHASES = 15
SLOTS = SIDE - 1 + 3
LOAD_UNITS, LOAD_LABELS, LOAD_MASK, STORE_OWN = range(4)


def spread_kernel(
    mask_hbm,
    emb_hbm,
    lab_hbm,
    out_hbm,
    mask_ref,
    emb_ref,
    uj,
    ui,
    kmat,
    lab,
    sc1,
    sc2,
    part1,
    part2,
    rcv1,
    rcv2,
    deg,
    fin,
    send_sem,
    recv_sem,
    local_sem,
):
    row = lax.axis_index("row")
    col = lax.axis_index("col")
    y = lax.div(row, 4)
    z_lo = lax.rem(row, 4)
    z_hi = lax.div(col, 8)
    c = lax.rem(col, 8)
    core = lax.rem(col, 2)
    z = z_hi * 4 + z_lo

    def at(new_y, new_z):
        return (new_y * 4 + lax.rem(new_z, 4), lax.div(new_z, 4) * 8 + c)

    def gather_peer(k):
        return at(lax.rem(y + core * k, SIDE), lax.rem(z + (1 - core) * k, SIDE))

    def reduce_peer(k):
        return at(lax.rem(y + (1 - core) * k, SIDE), lax.rem(z + core * k, SIDE))

    def swap_index(k):
        return lax.rem(c + k, SIDE)

    def swap_peer(k):
        return (row, z_hi * 8 + swap_index(k))

    partner_c = c + 1 - 2 * core
    partner = (row, z_hi * 8 + partner_c)

    def beside(position):
        return (position[0], lax.div(position[1], 8) * 8 + partner_c)

    def cross_peer(k):
        return beside(reduce_peer(k))

    def x_peer(k):
        return swap_peer(2 * k)

    own_rows = pl.ds(pl.multiple_of(c * PIECE, PIECE), PIECE)
    own_lanes = pl.ds(pl.multiple_of(c * LANES, LANES), LANES)

    def local(slot, src, dst):
        copy = pltpu.make_async_copy(src, dst, local_sem.at[slot])
        copy.start()
        return copy

    load_units = local(LOAD_UNITS, emb_hbm, emb_ref)
    load_labels = local(LOAD_LABELS, lab_hbm.at[:, own_lanes], lab.at[0, own_rows, :])
    load_mask = local(LOAD_MASK, mask_hbm, mask_ref)
    barrier = pltpu.get_barrier_semaphore()
    for k in range(1, SIDE):
        for peer in (gather_peer(k), reduce_peer(k), swap_peer(k), beside(gather_peer(k))):
            pl.semaphore_signal(barrier, inc=1, device_id=peer, device_id_type=MESH)

    def describe(phase, src, dst, device, slot=None):
        return pltpu.make_async_remote_copy(
            src_ref=src,
            dst_ref=dst,
            send_sem=send_sem.at[phase],
            recv_sem=recv_sem.at[phase if slot is None else PHASES + slot],
            device_id=device,
            device_id_type=MESH,
        )

    def send(phase, src, dst, device, slot=None):
        copy = describe(phase, src, dst, device, slot)
        copy.start()
        return copy

    sent = []

    def whole(phase, ref):
        copy = describe(phase, ref, ref, partner)
        sent.append(copy)
        return copy

    low, high = slice(0, LANES), slice(LANES, 2 * LANES)
    load_units.wait()
    values = emb_ref[...].astype(jnp.float32)
    norm = lax.rsqrt(jnp.sum(values * values, axis=1, keepdims=True) + EPSILON)
    uj[0, own_rows, :] = (values * norm).astype(jnp.bfloat16)

    pl.semaphore_wait(barrier, 4 * (SIDE - 1))

    for k in range(1, SIDE):
        send(UNIT_SWAP, uj.at[0, own_rows, low], uj.at[0, own_rows, low], swap_peer(k))
    piece = uj.at[0, own_rows, high]
    for k in FAR_FIRST:
        send(PIECE_GATHER, piece, uj.at[k, own_rows, high], gather_peer(k))
        send(PIECE_GATHER, piece, uj.at[k, own_rows, high], cross_peer(k))
    send(PIECE_GATHER, piece, piece, partner)
    for k in range(1, SIDE):
        lanes = pl.ds(pl.multiple_of(swap_index(k) * LANES, LANES), LANES)
        send(LABEL_SWAP, lab_hbm.at[:, lanes], lab.at[0, own_rows, :], swap_peer(k))

    others = slice(1, SIDE)
    whole(UNIT_SWAP, uj.at[0, 0 : (SIDE - 1) * PIECE, low]).wait_recv()
    unit_gathers = {
        k: send(UNIT_GATHER, uj.at[0, :, low], uj.at[k, :, low], gather_peer(k), slot=k - 1)
        for k in FAR_FIRST
    }
    whole(UNIT_GATHER, uj.at[others, :, low])
    whole(PIECE_GATHER, uj.at[0:5, 0 : 3 * PIECE, low]).wait_recv()
    pair = lax.div(c, 2) * 2 * PIECE

    def pair_rows(start):
        return pl.ds(pl.multiple_of(start, 2 * PIECE), 2 * PIECE)

    block = uj.at[:, pair_rows(pair), high]
    crosses = {k: send(CROSS, block, block, x_peer(k), slot=SIDE - 2 + k) for k in (2, 1, 3)}
    whole(CROSS, uj.at[:, 0 : 6 * PIECE, high])

    def pass_pair(start):
        send(UNIT_PASS, uj.at[others, pair_rows(start), high], ui.at[others, pair_rows(start), high], partner)

    pass_pair(pair)
    load_labels.wait()
    whole(LABEL_SWAP, lab.at[0, 0 : (SIDE - 1) * PIECE, :]).wait_recv()
    for k in FAR_FIRST:
        send(LABEL_GATHER, lab.at[0], lab.at[k], gather_peer(k))
    for k in NEAR_FIRST:
        unit_gathers[k].wait_recv()
        send(UNIT_PASS, uj.at[k, :, low], ui.at[k, :, low], partner)
    for k in (1, 3, 2):
        crosses[k].wait_recv()
        pass_pair(lax.rem(pair + (4 - k) * 2 * PIECE, CHUNK))
    ui[0] = uj[0]
    whole(UNIT_PASS, ui.at[others]).wait_recv()
    load_mask.wait()

    scale = SHARPNESS * math.sqrt(emb_ref.shape[1]) * math.log2(math.e)
    lane = lax.broadcasted_iota(jnp.int32, (1, 2 * CHUNK), 1)

    def block_of(chunk_y, chunk_z):
        return chunk_y * 4 + lax.rem(chunk_z, 4)

    def back(position, k):
        return lax.rem(position + SIDE - k, SIDE)

    def kept(row_block, col_block):
        low = jnp.minimum(row_block, col_block)
        high = jnp.maximum(row_block, col_block)
        return jnp.where(row_block == col_block, 1, mask_ref[low, high]).astype(jnp.float32)

    def make_columns(group, carry):
        columns = uj[pl.ds(2 * group, 2)].reshape(2 * CHUNK, emb_ref.shape[1])
        col_blocks = [
            block_of(back(y, core * (2 * group + half)), back(z, (1 - core) * (2 * group + half)))
            for half in range(2)
        ]
        sums = jnp.zeros((1, 2 * CHUNK), jnp.float32)
        for k in range(SIDE):
            row_block = block_of(back(y, (1 - core) * k), back(z, core * k))
            cosine = lax.dot_general(
                ui[k], columns, (((1,), (1,)), ((), ())), preferred_element_type=jnp.float32
            )
            keep = jnp.where(
                lane < CHUNK, kept(row_block, col_blocks[0]), kept(row_block, col_blocks[1])
            )
            weights = jnp.exp2(cosine * scale) * keep
            if k == 0:
                own_row = lax.broadcasted_iota(jnp.int32, weights.shape, 0)
                own_col = lax.broadcasted_iota(jnp.int32, weights.shape, 1) + group * (2 * CHUNK)
                weights = jnp.where(own_row == own_col, 0.0, weights)
            weights = weights.astype(jnp.bfloat16)
            kmat[k, :, pl.ds(pl.multiple_of(group * 2 * CHUNK, 2 * CHUNK), 2 * CHUNK)] = weights
            sums = sums + jnp.sum(weights.astype(jnp.float32), axis=0, keepdims=True)
        deg[0, pl.ds(2 * group, 1), :] = sums[:, :CHUNK]
        deg[0, pl.ds(2 * group + 1, 1), :] = sums[:, CHUNK:]
        return carry

    lax.fori_loop(0, SIDE // 2, make_columns, 0)

    for k in FAR_FIRST:
        send(DEGREE, deg.at[0], deg.at[k], gather_peer(k))
    whole(LABEL_GATHER, lab.at[others]).wait_recv()
    whole(DEGREE, deg.at[others]).wait_recv()
    degree = deg[0]
    for k in range(1, SIDE):
        degree = degree + pltpu.roll(deg[k], k, 0)
    inv_root = jnp.transpose(lax.rsqrt(degree))
    for k in range(SIDE):
        sc1[k] = (lab[k].astype(jnp.float32) * inv_root[:, k : k + 1]).astype(jnp.bfloat16)
    own_root = inv_root[:, 0:1]
    seeds = lab[0].astype(jnp.float32)

    def rows_of(half):
        return pl.ds(half * HALF, HALF)

    def iterate(phases, scaled, part, rcv, finish):
        spreads = []
        for half in range(2):
            rows = rows_of(half)
            spread = jnp.dot(
                kmat[:, rows, :].reshape(SIDE * HALF, SIDE * CHUNK),
                scaled[...].reshape(SIDE * CHUNK, LANES),
                preferred_element_type=jnp.float32,
            ).reshape(SIDE, HALF, LANES)
            spreads.append(spread[0])
            for k in FAR_FIRST:
                part[k, rows, :] = spread[k].astype(jnp.bfloat16)
            for k in FAR_FIRST:
                send(phases[half], part.at[k, rows, :], rcv.at[k, rows, :], reduce_peer(SIDE - k))
        for half in range(2):
            whole(phases[half], rcv.at[others, rows_of(half), :]).wait_recv()
            total = spreads[half]
            for k in range(1, SIDE):
                total = total + rcv[k, rows_of(half), :].astype(jnp.float32)
            rows = slice(half * HALF, (half + 1) * HALF)
            finish(half, MIXING * own_root[rows] * total + (1.0 - MIXING) * seeds[rows])

    def finish_first(half, current):
        rows = rows_of(half)
        root = own_root[half * HALF : (half + 1) * HALF]
        sc2[0, rows, :] = (root * current).astype(jnp.bfloat16)
        for k in FAR_FIRST:
            send(GATHER2[half], sc2.at[0, rows, :], sc2.at[k, rows, :], gather_peer(k))

    def finish_last(half, current):
        fin[rows_of(half), :] = current.astype(jnp.bfloat16)

    iterate(REDUCE1, sc1, part1, rcv1, finish_first)
    for half in range(2):
        whole(GATHER2[half], sc2.at[others, rows_of(half), :]).wait_recv()
    iterate(REDUCE2, sc2, part2, rcv2, finish_last)
    store_own = local(STORE_OWN, fin.at[own_rows, :], out_hbm.at[:, own_lanes])
    for k in range(1, SIDE):
        rows = pl.ds(pl.multiple_of(swap_index(k) * PIECE, PIECE), PIECE)
        send(FINAL, fin.at[rows, :], out_hbm.at[:, own_lanes], swap_peer(k))
    whole(FINAL, fin.at[0 : (SIDE - 1) * PIECE, :]).wait_recv()
    store_own.wait()
    for copy in sent:
        copy.wait_send()


def shards(embeddings, labels, tile_mask):
    width = embeddings.shape[1]
    anywhere = pl.BlockSpec(memory_space=pl.ANY)
    units = pltpu.VMEM((SIDE, CHUNK, width), jnp.bfloat16)
    chunks = pltpu.VMEM((SIDE, CHUNK, LANES), jnp.bfloat16)
    return pl.pallas_call(
        spread_kernel,
        out_shape=jax.ShapeDtypeStruct(labels.shape, jnp.bfloat16),
        in_specs=[anywhere] * 3,
        out_specs=anywhere,
        scratch_shapes=[
            pltpu.SMEM(tile_mask.shape, jnp.int32),
            pltpu.VMEM(embeddings.shape, jnp.bfloat16),
            units,
            units,
            pltpu.VMEM((SIDE, CHUNK, SIDE * CHUNK), jnp.bfloat16),
            chunks,
            chunks,
            chunks,
            chunks,
            chunks,
            chunks,
            chunks,
            pltpu.VMEM((SIDE, SIDE, CHUNK), jnp.float32),
            pltpu.VMEM((CHUNK, LANES), jnp.bfloat16),
            pltpu.SemaphoreType.DMA((PHASES,)),
            pltpu.SemaphoreType.DMA((PHASES + SLOTS,)),
            pltpu.SemaphoreType.DMA((4,)),
        ],
        compiler_params=pltpu.CompilerParams(collective_id=0, has_side_effects=True),
    )(tile_mask, embeddings, labels)


def solution(mesh):
    placed = (P(("row", "col"), None), P(("row", "col"), None), P())
    return jax.shard_map(
        shards, mesh=mesh, in_specs=placed, out_specs=P(("row", "col"), None), check_vma=False
    )
```

```python
import math

import jax
import jax.numpy as jnp
from jax import lax
from jax.experimental import pallas as pl
from jax.experimental.pallas import tpu as pltpu
from jax.sharding import PartitionSpec as P

MIXING = 0.9
SHARPNESS = 3.0
EPSILON = 1e-06

SIDE = 8
CHUNK = 128
PIECE = 16
LANES = 128
MESH = pl.DeviceIdType.MESH
FAR_FIRST = (4, 3, 5, 2, 6, 1, 7)
NEAR_FIRST = (1, 7, 2, 6, 3, 5, 4)

HALF = CHUNK // 2
UNIT_SWAP, LABEL_SWAP, UNIT_GATHER, UNIT_PASS, LABEL_GATHER, DEGREE = range(6)
REDUCE1, GATHER2 = (6, 7), (8, 9)
REDUCE2, OWN_REDUCE2, PIECE_GATHER, CROSS = 10, 11, 12, 13
PHASES = 14
SLOTS = SIDE - 1 + 3
LOAD_UNITS, LOAD_LABELS, LOAD_MASK, STORE_ROOT, STORE_OWN = range(5)


def spread_kernel(
    mask_hbm,
    emb_hbm,
    lab_hbm,
    parts_hbm,
    root_hbm,
    mask_ref,
    emb_ref,
    uj,
    ui,
    kmat,
    lab,
    sc1,
    sc2,
    part1,
    part2,
    rcv1,
    deg,
    root,
    root_wide,
    send_sem,
    recv_sem,
    local_sem,
):
    row = lax.axis_index("row")
    col = lax.axis_index("col")
    y = lax.div(row, 4)
    z_lo = lax.rem(row, 4)
    z_hi = lax.div(col, 8)
    c = lax.rem(col, 8)
    core = lax.rem(col, 2)
    z = z_hi * 4 + z_lo

    def at(new_y, new_z):
        return (new_y * 4 + lax.rem(new_z, 4), lax.div(new_z, 4) * 8 + c)

    def gather_peer(k):
        return at(lax.rem(y + core * k, SIDE), lax.rem(z + (1 - core) * k, SIDE))

    def reduce_peer(k):
        return at(lax.rem(y + (1 - core) * k, SIDE), lax.rem(z + core * k, SIDE))

    def swap_index(k):
        return lax.rem(c + k, SIDE)

    def swap_peer(k):
        return (row, z_hi * 8 + swap_index(k))

    partner_c = c + 1 - 2 * core
    partner = (row, z_hi * 8 + partner_c)

    def beside(position):
        return (position[0], lax.div(position[1], 8) * 8 + partner_c)

    def cross_peer(k):
        return beside(reduce_peer(k))

    def x_peer(k):
        return swap_peer(2 * k)

    own_rows = pl.ds(pl.multiple_of(c * PIECE, PIECE), PIECE)
    own_lanes = pl.ds(pl.multiple_of(c * LANES, LANES), LANES)

    def local(slot, src, dst):
        copy = pltpu.make_async_copy(src, dst, local_sem.at[slot])
        copy.start()
        return copy

    load_units = local(LOAD_UNITS, emb_hbm, emb_ref)
    load_labels = local(LOAD_LABELS, lab_hbm.at[:, own_lanes], lab.at[0, own_rows, :])
    load_mask = local(LOAD_MASK, mask_hbm, mask_ref)
    barrier = pltpu.get_barrier_semaphore()
    for k in range(1, SIDE):
        for peer in (gather_peer(k), reduce_peer(k), swap_peer(k), beside(gather_peer(k))):
            pl.semaphore_signal(barrier, inc=1, device_id=peer, device_id_type=MESH)

    def describe(phase, src, dst, device, slot=None):
        return pltpu.make_async_remote_copy(
            src_ref=src,
            dst_ref=dst,
            send_sem=send_sem.at[phase],
            recv_sem=recv_sem.at[phase if slot is None else PHASES + slot],
            device_id=device,
            device_id_type=MESH,
        )

    def send(phase, src, dst, device, slot=None):
        copy = describe(phase, src, dst, device, slot)
        copy.start()
        return copy

    sent = []

    def whole(phase, ref):
        copy = describe(phase, ref, ref, partner)
        sent.append(copy)
        return copy

    low, high = slice(0, LANES), slice(LANES, 2 * LANES)
    load_units.wait()
    values = emb_ref[...].astype(jnp.float32)
    norm = lax.rsqrt(jnp.sum(values * values, axis=1, keepdims=True) + EPSILON)
    uj[0, own_rows, :] = (values * norm).astype(jnp.bfloat16)

    pl.semaphore_wait(barrier, 4 * (SIDE - 1))

    for k in range(1, SIDE):
        send(UNIT_SWAP, uj.at[0, own_rows, low], uj.at[0, own_rows, low], swap_peer(k))
    piece = uj.at[0, own_rows, high]
    for k in FAR_FIRST:
        send(PIECE_GATHER, piece, uj.at[k, own_rows, high], gather_peer(k))
        send(PIECE_GATHER, piece, uj.at[k, own_rows, high], cross_peer(k))
    send(PIECE_GATHER, piece, piece, partner)
    for k in range(1, SIDE):
        lanes = pl.ds(pl.multiple_of(swap_index(k) * LANES, LANES), LANES)
        send(LABEL_SWAP, lab_hbm.at[:, lanes], lab.at[0, own_rows, :], swap_peer(k))

    others = slice(1, SIDE)
    whole(UNIT_SWAP, uj.at[0, 0 : (SIDE - 1) * PIECE, low]).wait_recv()
    unit_gathers = {
        k: send(UNIT_GATHER, uj.at[0, :, low], uj.at[k, :, low], gather_peer(k), slot=k - 1)
        for k in FAR_FIRST
    }
    whole(UNIT_GATHER, uj.at[others, :, low])
    whole(PIECE_GATHER, uj.at[0:5, 0 : 3 * PIECE, low]).wait_recv()
    pair = lax.div(c, 2) * 2 * PIECE

    def pair_rows(start):
        return pl.ds(pl.multiple_of(start, 2 * PIECE), 2 * PIECE)

    block = uj.at[:, pair_rows(pair), high]
    crosses = {k: send(CROSS, block, block, x_peer(k), slot=SIDE - 2 + k) for k in (2, 1, 3)}
    whole(CROSS, uj.at[:, 0 : 6 * PIECE, high])

    def pass_pair(start):
        send(UNIT_PASS, uj.at[others, pair_rows(start), high], ui.at[others, pair_rows(start), high], partner)

    pass_pair(pair)
    load_labels.wait()
    whole(LABEL_SWAP, lab.at[0, 0 : (SIDE - 1) * PIECE, :]).wait_recv()
    for k in FAR_FIRST:
        send(LABEL_GATHER, lab.at[0], lab.at[k], gather_peer(k))
    for k in NEAR_FIRST:
        unit_gathers[k].wait_recv()
        send(UNIT_PASS, uj.at[k, :, low], ui.at[k, :, low], partner)
    for k in (1, 3, 2):
        crosses[k].wait_recv()
        pass_pair(lax.rem(pair + (4 - k) * 2 * PIECE, CHUNK))
    scale = SHARPNESS * math.sqrt(emb_ref.shape[1]) * math.log2(math.e)
    lane = lax.broadcasted_iota(jnp.int32, (1, 2 * CHUNK), 1)

    def block_of(chunk_y, chunk_z):
        return chunk_y * 4 + lax.rem(chunk_z, 4)

    def back(position, k):
        return lax.rem(position + SIDE - k, SIDE)

    def kept(row_block, col_block):
        low = jnp.minimum(row_block, col_block)
        high = jnp.maximum(row_block, col_block)
        return jnp.where(row_block == col_block, 1, mask_ref[low, high]).astype(jnp.float32)

    groups = range(SIDE // 2)
    col_blocks = [block_of(back(y, core * k), back(z, (1 - core) * k)) for k in range(SIDE)]
    row_blocks = [block_of(back(y, (1 - core) * k), back(z, core * k)) for k in range(SIDE)]

    def make_tile(vecs, k, group):
        cosine = lax.dot_general(
            vecs[k],
            uj[2 * group : 2 * group + 2].reshape(2 * CHUNK, emb_ref.shape[1]),
            (((1,), (1,)), ((), ())),
            preferred_element_type=jnp.float32,
        )
        keep = jnp.where(
            lane < CHUNK,
            kept(row_blocks[k], col_blocks[2 * group]),
            kept(row_blocks[k], col_blocks[2 * group + 1]),
        )
        weights = jnp.exp2(cosine * scale)
        if k == 0 and group == 0:
            own_row = lax.broadcasted_iota(jnp.int32, weights.shape, 0)
            own_col = lax.broadcasted_iota(jnp.int32, weights.shape, 1)
            weights = jnp.where(own_row == own_col, 0.0, weights)
        kmat[k, :, 2 * CHUNK * group : 2 * CHUNK * (group + 1)] = weights.astype(
            jnp.bfloat16
        ) * keep.astype(jnp.bfloat16)
        return jnp.sum(weights, axis=0, keepdims=True) * keep

    load_mask.wait()
    sums = [make_tile(uj, 0, group) for group in groups]
    whole(UNIT_PASS, ui.at[others]).wait_recv()
    for group in groups:
        for k in range(1, SIDE):
            sums[group] = sums[group] + make_tile(ui, k, group)
        deg[0, 2 * group : 2 * group + 1, :] = sums[group][:, :CHUNK]
        deg[0, 2 * group + 1 : 2 * group + 2, :] = sums[group][:, CHUNK:]
    for k in FAR_FIRST:
        send(DEGREE, deg.at[0], deg.at[k], gather_peer(k))
    whole(LABEL_GATHER, lab.at[others]).wait_recv()
    whole(DEGREE, deg.at[others]).wait_recv()
    degree = deg[0]
    for k in range(1, SIDE):
        degree = degree + pltpu.roll(deg[k], k, 0)
    inv_root = jnp.transpose(lax.rsqrt(degree))
    for k in range(SIDE):
        sc1[k] = (lab[k].astype(jnp.float32) * inv_root[:, k : k + 1]).astype(jnp.bfloat16)
    own_root = inv_root[:, 0:1]
    seeds = lab[0].astype(jnp.float32)

    def rows_of(half):
        return pl.ds(half * HALF, HALF)

    def spread_half(scaled, part, half):
        rows = rows_of(half)
        spread = jnp.dot(
            kmat[:, rows, :].reshape(SIDE * HALF, SIDE * CHUNK),
            scaled[...].reshape(SIDE * CHUNK, LANES),
            preferred_element_type=jnp.float32,
        ).reshape(SIDE, HALF, LANES)
        part[:, rows, :] = spread.astype(jnp.bfloat16)
        return spread[0]

    spreads = []
    for half in range(2):
        rows = rows_of(half)
        spreads.append(spread_half(sc1, part1, half))
        for k in FAR_FIRST:
            send(REDUCE1[half], part1.at[k, rows, :], rcv1.at[k, rows, :], reduce_peer(SIDE - k))
    root[...] = jnp.broadcast_to(own_root, root.shape)
    for half in range(2):
        rows = rows_of(half)
        picked = slice(half * HALF, (half + 1) * HALF)
        whole(REDUCE1[half], rcv1.at[others, rows, :]).wait_recv()
        total = spreads[half]
        for k in range(1, SIDE):
            total = total + rcv1[k, rows, :].astype(jnp.float32)
        current = MIXING * own_root[picked] * total + (1.0 - MIXING) * seeds[picked]
        sc2[0, rows, :] = (own_root[picked] * current).astype(jnp.bfloat16)
        for k in FAR_FIRST:
            send(GATHER2[half], sc2.at[0, rows, :], sc2.at[k, rows, :], gather_peer(k))
    root_wide[...] = jnp.concatenate([root[own_rows, :]] * SIDE, axis=1)
    store_root = local(STORE_ROOT, root_wide, root_hbm)
    for half in range(2):
        whole(GATHER2[half], sc2.at[others, rows_of(half), :]).wait_recv()
    for half in range(2):
        spread_half(sc2, part2, half)
        for k in FAR_FIRST:
            new_row, new_col = reduce_peer(SIDE - k)
            first = lax.div(new_col, SIDE) * SIDE
            for member in range(half * SIDE // 2, (half + 1) * SIDE // 2):
                send(
                    REDUCE2,
                    part2.at[k, member * PIECE : (member + 1) * PIECE, :],
                    parts_hbm.at[k, :, own_lanes],
                    (new_row, first + member),
                )
    for k in range(1, SIDE):
        rows = pl.ds(pl.multiple_of(swap_index(k) * PIECE, PIECE), PIECE)
        send(OWN_REDUCE2, part2.at[0, rows, :], parts_hbm.at[0, :, own_lanes], swap_peer(k))
    store_own = local(STORE_OWN, part2.at[0, own_rows, :], parts_hbm.at[0, :, own_lanes])
    store_root.wait()
    store_own.wait()
    whole(OWN_REDUCE2, rcv1.at[0, 0 : (SIDE - 1) * PIECE, :]).wait_recv()
    whole(REDUCE2, rcv1.at[others]).wait_recv()
    for copy in sent:
        copy.wait_send()


def shards(embeddings, labels, tile_mask):
    width = embeddings.shape[1]
    anywhere = pl.BlockSpec(memory_space=pl.ANY)
    units = pltpu.VMEM((SIDE, CHUNK, width), jnp.bfloat16)
    chunks = pltpu.VMEM((SIDE, CHUNK, LANES), jnp.bfloat16)
    parts, root = pl.pallas_call(
        spread_kernel,
        out_shape=(
            jax.ShapeDtypeStruct((SIDE, *labels.shape), jnp.bfloat16),
            jax.ShapeDtypeStruct(labels.shape, jnp.float32),
        ),
        in_specs=[anywhere] * 3,
        out_specs=(anywhere, anywhere),
        scratch_shapes=[
            pltpu.SMEM(tile_mask.shape, jnp.int32),
            pltpu.VMEM(embeddings.shape, jnp.bfloat16),
            units,
            units,
            pltpu.VMEM((SIDE, CHUNK, SIDE * CHUNK), jnp.bfloat16),
            chunks,
            chunks,
            chunks,
            chunks,
            chunks,
            chunks,
            pltpu.VMEM((SIDE, SIDE, CHUNK), jnp.float32),
            pltpu.VMEM((CHUNK, LANES), jnp.float32),
            pltpu.VMEM(labels.shape, jnp.float32),
            pltpu.SemaphoreType.DMA((PHASES,)),
            pltpu.SemaphoreType.DMA((PHASES + SLOTS,)),
            pltpu.SemaphoreType.DMA((5,)),
        ],
        compiler_params=pltpu.CompilerParams(collective_id=0, has_side_effects=True),
    )(tile_mask, embeddings, labels)
    spread = parts[0].astype(jnp.float32)
    for k in range(1, SIDE):
        spread = spread + parts[k].astype(jnp.float32)
    current = MIXING * root * spread + (1.0 - MIXING) * labels.astype(jnp.float32)
    return current.astype(jnp.bfloat16)


def solution(mesh):
    placed = (P(("row", "col"), None), P(("row", "col"), None), P())
    return jax.shard_map(
        shards, mesh=mesh, in_specs=placed, out_specs=P(("row", "col"), None), check_vma=False
    )
```

```python
import math

import jax
import jax.numpy as jnp
from jax import lax
from jax.experimental import pallas as pl
from jax.experimental.pallas import tpu as pltpu
from jax.sharding import PartitionSpec as P

MIXING = 0.9
SHARPNESS = 3.0
EPSILON = 1e-06

SIDE = 8
CHUNK = 128
PIECE = 16
LANES = 128
MESH = pl.DeviceIdType.MESH
FAR_FIRST = (4, 3, 5, 2, 6, 1, 7)
NEAR_FIRST = (1, 7, 2, 6, 3, 5, 4)

HALF = CHUNK // 2
UNIT_SWAP, LABEL_SWAP, UNIT_GATHER, UNIT_PASS, LABEL_GATHER, DEGREE = range(6)
REDUCE1, GATHER2 = (6, 7), (8, 9)
REDUCE2, OWN_REDUCE2, PIECE_GATHER, CROSS = 10, 11, 12, 13
PHASES = 14
SLOTS = SIDE - 1 + 3
LOAD_UNITS, LOAD_LABELS, LOAD_MASK, STORE_ROOT, STORE_OWN = range(5)


def spread_kernel(
    mask_hbm,
    emb_hbm,
    lab_hbm,
    parts_hbm,
    root_hbm,
    mask_ref,
    emb_ref,
    uj,
    ui,
    kmat,
    lab,
    sc1,
    sc2,
    part1,
    part2,
    rcv1,
    acc,
    deg,
    root,
    root_wide,
    send_sem,
    recv_sem,
    local_sem,
):
    row = lax.axis_index("row")
    col = lax.axis_index("col")
    y = lax.div(row, 4)
    z_lo = lax.rem(row, 4)
    z_hi = lax.div(col, 8)
    c = lax.rem(col, 8)
    core = lax.rem(col, 2)
    z = z_hi * 4 + z_lo

    def at(new_y, new_z):
        return (new_y * 4 + lax.rem(new_z, 4), lax.div(new_z, 4) * 8 + c)

    def gather_peer(k):
        return at(lax.rem(y + core * k, SIDE), lax.rem(z + (1 - core) * k, SIDE))

    def reduce_peer(k):
        return at(lax.rem(y + (1 - core) * k, SIDE), lax.rem(z + core * k, SIDE))

    def swap_index(k):
        return lax.rem(c + k, SIDE)

    def swap_peer(k):
        return (row, z_hi * 8 + swap_index(k))

    partner_c = c + 1 - 2 * core
    partner = (row, z_hi * 8 + partner_c)

    def beside(position):
        return (position[0], lax.div(position[1], 8) * 8 + partner_c)

    def cross_peer(k):
        return beside(reduce_peer(k))

    def x_peer(k):
        return swap_peer(2 * k)

    own_rows = pl.ds(pl.multiple_of(c * PIECE, PIECE), PIECE)
    own_lanes = pl.ds(pl.multiple_of(c * LANES, LANES), LANES)

    def local(slot, src, dst):
        copy = pltpu.make_async_copy(src, dst, local_sem.at[slot])
        copy.start()
        return copy

    load_units = local(LOAD_UNITS, emb_hbm, emb_ref)
    load_labels = local(LOAD_LABELS, lab_hbm.at[:, own_lanes], lab.at[0, own_rows, :])
    load_mask = local(LOAD_MASK, mask_hbm, mask_ref)
    barrier = pltpu.get_barrier_semaphore()
    for k in range(1, SIDE):
        for peer in (gather_peer(k), swap_peer(k), beside(gather_peer(k))):
            pl.semaphore_signal(barrier, inc=1, device_id=peer, device_id_type=MESH)

    def describe(phase, src, dst, device, slot=None):
        return pltpu.make_async_remote_copy(
            src_ref=src,
            dst_ref=dst,
            send_sem=send_sem.at[phase],
            recv_sem=recv_sem.at[phase if slot is None else PHASES + slot],
            device_id=device,
            device_id_type=MESH,
        )

    def send(phase, src, dst, device, slot=None):
        copy = describe(phase, src, dst, device, slot)
        copy.start()
        return copy

    sent = []

    def whole(phase, ref):
        copy = describe(phase, ref, ref, partner)
        sent.append(copy)
        return copy

    low, high = slice(0, LANES), slice(LANES, 2 * LANES)
    load_units.wait()
    values = emb_ref[...].astype(jnp.float32)
    norm = lax.rsqrt(jnp.sum(values * values, axis=1, keepdims=True) + EPSILON)
    uj[0, own_rows, :] = (values * norm).astype(jnp.bfloat16)

    pl.semaphore_wait(barrier, 3 * (SIDE - 1))

    for k in range(1, SIDE):
        send(UNIT_SWAP, uj.at[0, own_rows, low], uj.at[0, own_rows, low], swap_peer(k))
    piece = uj.at[0, own_rows, high]
    for k in FAR_FIRST:
        send(PIECE_GATHER, piece, uj.at[k, own_rows, high], gather_peer(k))
        send(PIECE_GATHER, piece, uj.at[k, own_rows, high], cross_peer(k))
    send(PIECE_GATHER, piece, piece, partner)
    for k in range(1, SIDE):
        lanes = pl.ds(pl.multiple_of(swap_index(k) * LANES, LANES), LANES)
        send(LABEL_SWAP, lab_hbm.at[:, lanes], lab.at[0, own_rows, :], swap_peer(k))

    others = slice(1, SIDE)
    whole(UNIT_SWAP, uj.at[0, 0 : (SIDE - 1) * PIECE, low]).wait_recv()
    unit_gathers = {
        k: send(UNIT_GATHER, uj.at[0, :, low], uj.at[k, :, low], gather_peer(k), slot=k - 1)
        for k in FAR_FIRST
    }
    whole(UNIT_GATHER, uj.at[others, :, low])
    whole(PIECE_GATHER, uj.at[0:5, 0 : 3 * PIECE, low]).wait_recv()
    pair = lax.div(c, 2) * 2 * PIECE

    def pair_rows(start):
        return pl.ds(pl.multiple_of(start, 2 * PIECE), 2 * PIECE)

    block = uj.at[:, pair_rows(pair), high]
    crosses = {k: send(CROSS, block, block, x_peer(k), slot=SIDE - 2 + k) for k in (2, 1, 3)}
    whole(CROSS, uj.at[:, 0 : 6 * PIECE, high])

    def pass_pair(start):
        send(UNIT_PASS, uj.at[others, pair_rows(start), high], ui.at[others, pair_rows(start), high], partner)

    pass_pair(pair)
    load_labels.wait()
    whole(LABEL_SWAP, lab.at[0, 0 : (SIDE - 1) * PIECE, :]).wait_recv()
    for k in FAR_FIRST:
        send(LABEL_GATHER, lab.at[0], lab.at[k], gather_peer(k))
    for k in NEAR_FIRST:
        unit_gathers[k].wait_recv()
        send(UNIT_PASS, uj.at[k, :, low], ui.at[k, :, low], partner)
    for k in (1, 3, 2):
        crosses[k].wait_recv()
        pass_pair(lax.rem(pair + (4 - k) * 2 * PIECE, CHUNK))
    scale = SHARPNESS * math.sqrt(emb_ref.shape[1]) * math.log2(math.e)
    lane = lax.broadcasted_iota(jnp.int32, (1, 2 * CHUNK), 1)

    def block_of(chunk_y, chunk_z):
        return chunk_y * 4 + lax.rem(chunk_z, 4)

    def back(position, k):
        return lax.rem(position + SIDE - k, SIDE)

    def kept(row_block, col_block):
        low = jnp.minimum(row_block, col_block)
        high = jnp.maximum(row_block, col_block)
        return jnp.where(row_block == col_block, 1, mask_ref[low, high]).astype(jnp.float32)

    col_blocks = [block_of(back(y, core * k), back(z, (1 - core) * k)) for k in range(SIDE)]
    row_blocks = [block_of(back(y, (1 - core) * k), back(z, core * k)) for k in range(SIDE)]

    def kept_lanes(k, quad):
        bits = [kept(row_blocks[k], col_blocks[4 * quad + j]) for j in range(4)]
        return jnp.where(
            lane < 2 * HALF,
            jnp.where(lane < HALF, bits[0], bits[1]),
            jnp.where(lane < 3 * HALF, bits[2], bits[3]),
        )

    def make_tile(vecs, k, half, quad, keep):
        cosine = lax.dot_general(
            vecs[k],
            uj[4 * quad : 4 * quad + 4, half * HALF : (half + 1) * HALF, :].reshape(
                4 * HALF, emb_ref.shape[1]
            ),
            (((1,), (1,)), ((), ())),
            preferred_element_type=jnp.float32,
        )
        weights = jnp.exp2(cosine * scale)
        if k == 0 and quad == 0:
            own_row = lax.broadcasted_iota(jnp.int32, weights.shape, 0)
            own_col = lax.broadcasted_iota(jnp.int32, weights.shape, 1)
            own = (own_col < HALF) & (own_row == own_col + half * HALF)
            weights = jnp.where(own, 0.0, weights)
        start = (2 * half + quad) * 4 * HALF
        kmat[k, :, start : start + 4 * HALF] = weights.astype(jnp.bfloat16) * keep.astype(
            jnp.bfloat16
        )
        return jnp.sum(weights, axis=0, keepdims=True) * keep

    load_mask.wait()
    sums = {}
    for quad in range(2):
        keep = kept_lanes(0, quad)
        for half in range(2):
            sums[half, quad] = make_tile(uj, 0, half, quad, keep)
    whole(UNIT_PASS, ui.at[others]).wait_recv()
    for quad in range(2):
        keeps = [kept_lanes(k, quad) for k in range(SIDE)]
        for half in range(2):
            for k in range(1, SIDE):
                sums[half, quad] = sums[half, quad] + make_tile(ui, k, half, quad, keeps[k])
        for j in range(4):
            lanes = slice(j * HALF, (j + 1) * HALF)
            deg[0, 4 * quad + j : 4 * quad + j + 1, :] = jnp.concatenate(
                [sums[0, quad][:, lanes], sums[1, quad][:, lanes]], axis=1
            )
    for k in FAR_FIRST:
        send(DEGREE, deg.at[0], deg.at[k], gather_peer(k))
    whole(LABEL_GATHER, lab.at[others]).wait_recv()
    whole(DEGREE, deg.at[others]).wait_recv()
    degree = deg[0]
    for k in range(1, SIDE):
        degree = degree + pltpu.roll(deg[k], k, 0)
    inv_root = jnp.transpose(lax.rsqrt(degree))
    for k in range(SIDE):
        scaled = (lab[k].astype(jnp.float32) * inv_root[:, k : k + 1]).astype(jnp.bfloat16)
        sc1[:, k] = scaled.reshape(2, HALF, LANES)
    own_root = inv_root[:, 0:1]
    seeds = lab[0].astype(jnp.float32)

    def rows_of(half):
        return pl.ds(half * HALF, HALF)

    def product(rows, lanes, scaled):
        matrix = kmat[:, rows, lanes]
        return jnp.dot(
            matrix.reshape(-1, matrix.shape[2]),
            scaled.reshape(-1, LANES),
            preferred_element_type=jnp.float32,
        ).reshape(SIDE, -1, LANES)

    spreads = []
    for half in range(2):
        rows = rows_of(half)
        spread = product(rows, slice(None), sc1[...])
        spreads.append(spread[0])
        part1[:, rows, :] = spread.astype(jnp.bfloat16)
        for k in FAR_FIRST:
            send(REDUCE1[half], part1.at[k, rows, :], rcv1.at[k, rows, :], reduce_peer(SIDE - k))
    root[...] = jnp.broadcast_to(own_root, root.shape)
    for half in range(2):
        rows = rows_of(half)
        picked = slice(half * HALF, (half + 1) * HALF)
        whole(REDUCE1[half], rcv1.at[others, rows, :]).wait_recv()
        total = spreads[half]
        for k in range(1, SIDE):
            total = total + rcv1[k, rows, :].astype(jnp.float32)
        current = MIXING * own_root[picked] * total + (1.0 - MIXING) * seeds[picked]
        sc2[half, 0] = (own_root[picked] * current).astype(jnp.bfloat16)
        for k in FAR_FIRST:
            send(GATHER2[half], sc2.at[half, 0], sc2.at[half, k], gather_peer(k))
    root_wide[...] = jnp.concatenate([root[own_rows, :]] * SIDE, axis=1)
    store_root = local(STORE_ROOT, root_wide, root_hbm)
    whole(GATHER2[0], sc2.at[0, others]).wait_recv()
    first_half, last_half = slice(0, SIDE * HALF), slice(SIDE * HALF, SIDE * CHUNK)
    acc[...] = product(slice(None), first_half, sc2[0])
    whole(GATHER2[1], sc2.at[1, others]).wait_recv()
    for half in range(2):
        rows = rows_of(half)
        spread = acc[:, rows, :] + product(rows, last_half, sc2[1])
        part2[:, rows, :] = spread.astype(jnp.bfloat16)
        for k in FAR_FIRST:
            new_row, new_col = reduce_peer(SIDE - k)
            first = lax.div(new_col, SIDE) * SIDE
            for member in range(half * SIDE // 2, (half + 1) * SIDE // 2):
                send(
                    REDUCE2,
                    part2.at[k, member * PIECE : (member + 1) * PIECE, :],
                    parts_hbm.at[k, :, own_lanes],
                    (new_row, first + member),
                )
    for k in range(1, SIDE):
        rows = pl.ds(pl.multiple_of(swap_index(k) * PIECE, PIECE), PIECE)
        send(OWN_REDUCE2, part2.at[0, rows, :], parts_hbm.at[0, :, own_lanes], swap_peer(k))
    store_own = local(STORE_OWN, part2.at[0, own_rows, :], parts_hbm.at[0, :, own_lanes])
    store_root.wait()
    store_own.wait()
    whole(OWN_REDUCE2, rcv1.at[0, 0 : (SIDE - 1) * PIECE, :]).wait_recv()
    whole(REDUCE2, rcv1.at[others]).wait_recv()
    for copy in sent:
        copy.wait_send()


def shards(embeddings, labels, tile_mask):
    width = embeddings.shape[1]
    anywhere = pl.BlockSpec(memory_space=pl.ANY)
    units = pltpu.VMEM((SIDE, CHUNK, width), jnp.bfloat16)
    chunks = pltpu.VMEM((SIDE, CHUNK, LANES), jnp.bfloat16)
    parts, root = pl.pallas_call(
        spread_kernel,
        out_shape=(
            jax.ShapeDtypeStruct((SIDE, *labels.shape), jnp.bfloat16),
            jax.ShapeDtypeStruct(labels.shape, jnp.float32),
        ),
        in_specs=[anywhere] * 3,
        out_specs=(anywhere, anywhere),
        scratch_shapes=[
            pltpu.SMEM(tile_mask.shape, jnp.int32),
            pltpu.VMEM(embeddings.shape, jnp.bfloat16),
            units,
            units,
            pltpu.VMEM((SIDE, CHUNK, SIDE * CHUNK), jnp.bfloat16),
            chunks,
            pltpu.VMEM((2, SIDE, HALF, LANES), jnp.bfloat16),
            pltpu.VMEM((2, SIDE, HALF, LANES), jnp.bfloat16),
            chunks,
            chunks,
            chunks,
            pltpu.VMEM((SIDE, CHUNK, LANES), jnp.float32),
            pltpu.VMEM((SIDE, SIDE, CHUNK), jnp.float32),
            pltpu.VMEM((CHUNK, LANES), jnp.float32),
            pltpu.VMEM(labels.shape, jnp.float32),
            pltpu.SemaphoreType.DMA((PHASES,)),
            pltpu.SemaphoreType.DMA((PHASES + SLOTS,)),
            pltpu.SemaphoreType.DMA((5,)),
        ],
        compiler_params=pltpu.CompilerParams(collective_id=0, has_side_effects=True),
    )(tile_mask, embeddings, labels)
    spread = parts[0].astype(jnp.float32)
    for k in range(1, SIDE):
        spread = spread + parts[k].astype(jnp.float32)
    current = MIXING * root * spread + (1.0 - MIXING) * labels.astype(jnp.float32)
    return current.astype(jnp.bfloat16)


def solution(mesh):
    placed = (P(("row", "col"), None), P(("row", "col"), None), P())
    return jax.shard_map(
        shards, mesh=mesh, in_specs=placed, out_specs=P(("row", "col"), None), check_vma=False
    )
```

```python
import math

import jax
import jax.numpy as jnp
from jax import lax
from jax.experimental import pallas as pl
from jax.experimental.pallas import tpu as pltpu
from jax.sharding import PartitionSpec as P

MIXING = 0.9
SHARPNESS = 3.0
EPSILON = 1e-06

SIDE = 8
CHUNK = 128
PIECE = 16
LANES = 128
MESH = pl.DeviceIdType.MESH
FAR_FIRST = (4, 3, 5, 2, 6, 1, 7)
NEAR_FIRST = (1, 7, 2, 6, 3, 5, 4)

HALF = CHUNK // 2
UNIT_SWAP, LABEL_SWAP, UNIT_GATHER, UNIT_PASS, LABEL_GATHER, DEGREE = range(6)
REDUCE1, GATHER2 = (6, 7), (8, 9)
REDUCE2, OWN_REDUCE2, PIECE_GATHER, CROSS = 10, 11, 12, 13
PHASES = 14
CROSS_SLOT = SIDE - 2
SWAP_SLOT = SIDE + 2
PIECE_SLOT = SIDE + 6
SLOTS = SIDE + 9
LOAD_UNITS, LOAD_LABELS, LOAD_MASK, STORE_ROOT, STORE_OWN = range(5)


def spread_kernel(
    mask_hbm,
    emb_hbm,
    lab_hbm,
    parts_hbm,
    root_hbm,
    mask_ref,
    emb_ref,
    uj,
    ui,
    kmat,
    lab,
    sc1,
    sc2,
    part1,
    part2,
    rcv1,
    acc,
    deg,
    root,
    root_wide,
    send_sem,
    recv_sem,
    local_sem,
):
    row = lax.axis_index("row")
    col = lax.axis_index("col")
    y = lax.div(row, 4)
    z_lo = lax.rem(row, 4)
    z_hi = lax.div(col, 8)
    c = lax.rem(col, 8)
    core = lax.rem(col, 2)
    z = z_hi * 4 + z_lo

    def at(new_y, new_z):
        return (new_y * 4 + lax.rem(new_z, 4), lax.div(new_z, 4) * 8 + c)

    def gather_peer(k):
        return at(lax.rem(y + core * k, SIDE), lax.rem(z + (1 - core) * k, SIDE))

    def reduce_peer(k):
        return at(lax.rem(y + (1 - core) * k, SIDE), lax.rem(z + core * k, SIDE))

    def swap_index(k):
        return lax.rem(c + k, SIDE)

    def swap_peer(k):
        return (row, z_hi * 8 + swap_index(k))

    partner_c = c + 1 - 2 * core
    partner = (row, z_hi * 8 + partner_c)

    def beside(position):
        return (position[0], lax.div(position[1], 8) * 8 + partner_c)

    def cross_peer(k):
        return beside(reduce_peer(k))

    def x_peer(k):
        return swap_peer(2 * k)

    own_rows = pl.ds(pl.multiple_of(c * PIECE, PIECE), PIECE)
    own_lanes = pl.ds(pl.multiple_of(c * LANES, LANES), LANES)

    def local(slot, src, dst):
        copy = pltpu.make_async_copy(src, dst, local_sem.at[slot])
        copy.start()
        return copy

    load_units = local(LOAD_UNITS, emb_hbm, emb_ref)
    load_labels = local(LOAD_LABELS, lab_hbm.at[:, own_lanes], lab.at[0, own_rows, :])
    load_mask = local(LOAD_MASK, mask_hbm, mask_ref)
    barrier = pltpu.get_barrier_semaphore()
    for k in range(1, SIDE):
        for peer in (gather_peer(k), swap_peer(k), beside(gather_peer(k))):
            pl.semaphore_signal(barrier, inc=1, device_id=peer, device_id_type=MESH)

    def describe(phase, src, dst, device, slot=None):
        return pltpu.make_async_remote_copy(
            src_ref=src,
            dst_ref=dst,
            send_sem=send_sem.at[phase],
            recv_sem=recv_sem.at[phase if slot is None else PHASES + slot],
            device_id=device,
            device_id_type=MESH,
        )

    def send(phase, src, dst, device, slot=None):
        copy = describe(phase, src, dst, device, slot)
        copy.start()
        return copy

    sent = []

    def whole(phase, ref):
        copy = describe(phase, ref, ref, partner)
        sent.append(copy)
        return copy

    low, high = slice(0, LANES), slice(LANES, 2 * LANES)
    load_units.wait()
    values = emb_ref[...].astype(jnp.float32)
    norm = lax.rsqrt(jnp.sum(values * values, axis=1, keepdims=True) + EPSILON)
    uj[0, own_rows, :] = (values * norm).astype(jnp.bfloat16)

    pl.semaphore_wait(barrier, 3 * (SIDE - 1))

    own_low = uj.at[0, own_rows, low]
    for k in (2, 1, 3):
        for peer in (x_peer(k), (row, z_hi * 8 + swap_index(2 * k) + 1 - 2 * core)):
            send(UNIT_SWAP, own_low, own_low, peer, slot=SWAP_SLOT + k)
    send(UNIT_SWAP, own_low, own_low, partner, slot=SWAP_SLOT)
    piece = uj.at[0, own_rows, high]
    group_of = {0: 0, 1: 0, 7: 0, 2: 1, 6: 1, 3: 2, 5: 2, 4: 2}
    for k in FAR_FIRST:
        for peer in (gather_peer(k), cross_peer(k)):
            slot = PIECE_SLOT + group_of[k]
            send(PIECE_GATHER, piece, uj.at[k, own_rows, high], peer, slot=slot)
    send(PIECE_GATHER, piece, piece, partner, slot=PIECE_SLOT)
    for k in range(1, SIDE):
        lanes = pl.ds(pl.multiple_of(swap_index(k) * LANES, LANES), LANES)
        send(LABEL_SWAP, lab_hbm.at[:, lanes], lab.at[0, own_rows, :], swap_peer(k))

    others = slice(1, SIDE)
    pair = lax.div(c, 2) * 2 * PIECE

    def pair_rows(k):
        start = lax.rem(pair + (4 - k) * 2 * PIECE, CHUNK)
        return pl.ds(pl.multiple_of(start, 2 * PIECE), 2 * PIECE)

    def gather_pair(x_back):
        count = 1 if x_back == 0 else 2
        region = uj.at[0, 0 : count * PIECE, low]
        describe(UNIT_SWAP, region, region, partner, slot=SWAP_SLOT + x_back).wait_recv()
        rows = pair_rows(x_back)
        for k in FAR_FIRST:
            send(UNIT_GATHER, uj.at[0, rows, low], uj.at[k, rows, low], gather_peer(k), slot=k - 1)

    def cross_group(group, count, slots):
        region = uj.at[0, 0 : count * PIECE, low]
        describe(PIECE_GATHER, region, region, partner, slot=PIECE_SLOT + group).wait_recv()
        for first, last in slots:
            block = uj.at[first:last, pair_rows(0), high]
            for k in (2, 1, 3):
                send(CROSS, block, block, x_peer(k), slot=CROSS_SLOT + k)

    def pass_pair(k):
        block = uj.at[others, pair_rows(k), high]
        send(UNIT_PASS, block, ui.at[others, pair_rows(k), high], partner)

    gather_pair(0)
    gather_pair(1)
    gather_pair(3)
    cross_group(0, 5, ((0, 2), (7, 8)))
    gather_pair(2)
    cross_group(1, 4, ((2, 3), (6, 7)))
    cross_group(2, 6, ((3, 6),))
    whole(UNIT_SWAP, uj.at[0, 0 : (SIDE - 1) * PIECE, low])
    whole(UNIT_GATHER, uj.at[others, :, low])
    whole(PIECE_GATHER, uj.at[0:5, 0 : 3 * PIECE, low])
    whole(CROSS, uj.at[:, 0 : 6 * PIECE, high])
    pass_pair(0)
    load_labels.wait()
    whole(LABEL_SWAP, lab.at[0, 0 : (SIDE - 1) * PIECE, :]).wait_recv()
    for k in FAR_FIRST:
        send(LABEL_GATHER, lab.at[0], lab.at[k], gather_peer(k))
    for k in NEAR_FIRST:
        describe(UNIT_GATHER, uj.at[k, :, low], uj.at[k, :, low], partner, slot=k - 1).wait_recv()
        send(UNIT_PASS, uj.at[k, :, low], ui.at[k, :, low], partner)
    for k in (1, 3, 2):
        block = uj.at[:, pair_rows(k), high]
        describe(CROSS, block, block, partner, slot=CROSS_SLOT + k).wait_recv()
        pass_pair(k)
    scale = SHARPNESS * math.sqrt(emb_ref.shape[1]) * math.log2(math.e)
    lane = lax.broadcasted_iota(jnp.int32, (1, 2 * CHUNK), 1)

    def block_of(chunk_y, chunk_z):
        return chunk_y * 4 + lax.rem(chunk_z, 4)

    def back(position, k):
        return lax.rem(position + SIDE - k, SIDE)

    def kept(row_block, col_block):
        low = jnp.minimum(row_block, col_block)
        high = jnp.maximum(row_block, col_block)
        return jnp.where(row_block == col_block, 1, mask_ref[low, high]).astype(jnp.float32)

    col_blocks = [block_of(back(y, core * k), back(z, (1 - core) * k)) for k in range(SIDE)]
    row_blocks = [block_of(back(y, (1 - core) * k), back(z, core * k)) for k in range(SIDE)]

    def kept_lanes(k, quad):
        bits = [kept(row_blocks[k], col_blocks[4 * quad + j]) for j in range(4)]
        return jnp.where(
            lane < 2 * HALF,
            jnp.where(lane < HALF, bits[0], bits[1]),
            jnp.where(lane < 3 * HALF, bits[2], bits[3]),
        )

    def make_tile(vecs, k, half, quad, keep):
        cosine = lax.dot_general(
            vecs[k],
            uj[4 * quad : 4 * quad + 4, half * HALF : (half + 1) * HALF, :].reshape(
                4 * HALF, emb_ref.shape[1]
            ),
            (((1,), (1,)), ((), ())),
            preferred_element_type=jnp.float32,
        )
        weights = jnp.exp2(cosine * scale)
        if k == 0 and quad == 0:
            own_row = lax.broadcasted_iota(jnp.int32, weights.shape, 0)
            own_col = lax.broadcasted_iota(jnp.int32, weights.shape, 1)
            own = (own_col < HALF) & (own_row == own_col + half * HALF)
            weights = jnp.where(own, 0.0, weights)
        start = (2 * half + quad) * 4 * HALF
        kmat[k, :, start : start + 4 * HALF] = weights.astype(jnp.bfloat16) * keep.astype(
            jnp.bfloat16
        )
        return jnp.sum(weights, axis=0, keepdims=True) * keep

    load_mask.wait()
    sums = {}
    for quad in range(2):
        keep = kept_lanes(0, quad)
        for half in range(2):
            sums[half, quad] = make_tile(uj, 0, half, quad, keep)
    whole(UNIT_PASS, ui.at[others]).wait_recv()
    for quad in range(2):
        keeps = [kept_lanes(k, quad) for k in range(SIDE)]
        for half in range(2):
            for k in range(1, SIDE):
                sums[half, quad] = sums[half, quad] + make_tile(ui, k, half, quad, keeps[k])
        for j in range(4):
            lanes = slice(j * HALF, (j + 1) * HALF)
            deg[0, 4 * quad + j : 4 * quad + j + 1, :] = jnp.concatenate(
                [sums[0, quad][:, lanes], sums[1, quad][:, lanes]], axis=1
            )
    for k in FAR_FIRST:
        send(DEGREE, deg.at[0], deg.at[k], gather_peer(k))
    whole(LABEL_GATHER, lab.at[others]).wait_recv()
    whole(DEGREE, deg.at[others]).wait_recv()
    degree = deg[0]
    for k in range(1, SIDE):
        degree = degree + pltpu.roll(deg[k], k, 0)
    inv_root = jnp.transpose(lax.rsqrt(degree))
    for k in range(SIDE):
        scaled = (lab[k].astype(jnp.float32) * inv_root[:, k : k + 1]).astype(jnp.bfloat16)
        sc1[:, k] = scaled.reshape(2, HALF, LANES)
    own_root = inv_root[:, 0:1]
    seeds = lab[0].astype(jnp.float32)

    def rows_of(half):
        return pl.ds(half * HALF, HALF)

    def product(rows, lanes, scaled):
        matrix = kmat[:, rows, lanes]
        return jnp.dot(
            matrix.reshape(-1, matrix.shape[2]),
            scaled.reshape(-1, LANES),
            preferred_element_type=jnp.float32,
        ).reshape(SIDE, -1, LANES)

    spreads = []
    for half in range(2):
        rows = rows_of(half)
        spread = product(rows, slice(None), sc1[...])
        spreads.append(spread[0])
        part1[:, rows, :] = spread.astype(jnp.bfloat16)
        for k in FAR_FIRST:
            send(REDUCE1[half], part1.at[k, rows, :], rcv1.at[k, rows, :], reduce_peer(SIDE - k))
    root[...] = jnp.broadcast_to(own_root, root.shape)
    for half in range(2):
        rows = rows_of(half)
        picked = slice(half * HALF, (half + 1) * HALF)
        whole(REDUCE1[half], rcv1.at[others, rows, :]).wait_recv()
        total = spreads[half]
        for k in range(1, SIDE):
            total = total + rcv1[k, rows, :].astype(jnp.float32)
        current = MIXING * own_root[picked] * total + (1.0 - MIXING) * seeds[picked]
        sc2[half, 0] = (own_root[picked] * current).astype(jnp.bfloat16)
        for k in FAR_FIRST:
            send(GATHER2[half], sc2.at[half, 0], sc2.at[half, k], gather_peer(k))
    root_wide[...] = jnp.concatenate([root[own_rows, :]] * SIDE, axis=1)
    store_root = local(STORE_ROOT, root_wide, root_hbm)
    whole(GATHER2[0], sc2.at[0, others]).wait_recv()
    first_half, last_half = slice(0, SIDE * HALF), slice(SIDE * HALF, SIDE * CHUNK)
    acc[...] = product(slice(None), first_half, sc2[0])
    whole(GATHER2[1], sc2.at[1, others]).wait_recv()
    for half in range(2):
        rows = rows_of(half)
        spread = acc[:, rows, :] + product(rows, last_half, sc2[1])
        part2[:, rows, :] = spread.astype(jnp.bfloat16)
        for k in FAR_FIRST:
            new_row, new_col = reduce_peer(SIDE - k)
            first = lax.div(new_col, SIDE) * SIDE
            for member in range(half * SIDE // 2, (half + 1) * SIDE // 2):
                send(
                    REDUCE2,
                    part2.at[k, member * PIECE : (member + 1) * PIECE, :],
                    parts_hbm.at[k, :, own_lanes],
                    (new_row, first + member),
                )
    for k in range(1, SIDE):
        rows = pl.ds(pl.multiple_of(swap_index(k) * PIECE, PIECE), PIECE)
        send(OWN_REDUCE2, part2.at[0, rows, :], parts_hbm.at[0, :, own_lanes], swap_peer(k))
    store_own = local(STORE_OWN, part2.at[0, own_rows, :], parts_hbm.at[0, :, own_lanes])
    store_root.wait()
    store_own.wait()
    whole(OWN_REDUCE2, rcv1.at[0, 0 : (SIDE - 1) * PIECE, :]).wait_recv()
    whole(REDUCE2, rcv1.at[others]).wait_recv()
    for copy in sent:
        copy.wait_send()


def shards(embeddings, labels, tile_mask):
    width = embeddings.shape[1]
    anywhere = pl.BlockSpec(memory_space=pl.ANY)
    units = pltpu.VMEM((SIDE, CHUNK, width), jnp.bfloat16)
    chunks = pltpu.VMEM((SIDE, CHUNK, LANES), jnp.bfloat16)
    parts, root = pl.pallas_call(
        spread_kernel,
        out_shape=(
            jax.ShapeDtypeStruct((SIDE, *labels.shape), jnp.bfloat16),
            jax.ShapeDtypeStruct(labels.shape, jnp.float32),
        ),
        in_specs=[anywhere] * 3,
        out_specs=(anywhere, anywhere),
        scratch_shapes=[
            pltpu.SMEM(tile_mask.shape, jnp.int32),
            pltpu.VMEM(embeddings.shape, jnp.bfloat16),
            units,
            units,
            pltpu.VMEM((SIDE, CHUNK, SIDE * CHUNK), jnp.bfloat16),
            chunks,
            pltpu.VMEM((2, SIDE, HALF, LANES), jnp.bfloat16),
            pltpu.VMEM((2, SIDE, HALF, LANES), jnp.bfloat16),
            chunks,
            chunks,
            chunks,
            pltpu.VMEM((SIDE, CHUNK, LANES), jnp.float32),
            pltpu.VMEM((SIDE, SIDE, CHUNK), jnp.float32),
            pltpu.VMEM((CHUNK, LANES), jnp.float32),
            pltpu.VMEM(labels.shape, jnp.float32),
            pltpu.SemaphoreType.DMA((PHASES,)),
            pltpu.SemaphoreType.DMA((PHASES + SLOTS,)),
            pltpu.SemaphoreType.DMA((5,)),
        ],
        compiler_params=pltpu.CompilerParams(collective_id=0, has_side_effects=True),
    )(tile_mask, embeddings, labels)
    spread = parts[0].astype(jnp.float32)
    for k in range(1, SIDE):
        spread = spread + parts[k].astype(jnp.float32)
    current = MIXING * root * spread + (1.0 - MIXING) * labels.astype(jnp.float32)
    return current.astype(jnp.bfloat16)


def solution(mesh):
    placed = (P(("row", "col"), None), P(("row", "col"), None), P())
    return jax.shard_map(
        shards, mesh=mesh, in_specs=placed, out_specs=P(("row", "col"), None), check_vma=False
    )
```

```python
import math

import jax
import jax.numpy as jnp
from jax import lax
from jax.experimental import pallas as pl
from jax.experimental.pallas import tpu as pltpu
from jax.sharding import PartitionSpec as P

MIXING = 0.9
SHARPNESS = 3.0
EPSILON = 1e-06

SIDE = 8
CHUNK = 128
PIECE = 16
LANES = 128
MESH = pl.DeviceIdType.MESH
FAR_FIRST = (4, 3, 5, 2, 6, 1, 7)
NEAR_FIRST = (1, 7, 2, 6, 3, 5, 4)

HALF = CHUNK // 2
UNIT_SWAP, LABEL_SWAP, UNIT_GATHER, UNIT_PASS, LABEL_GATHER = range(5)
REDUCE1, GATHER2 = (6, 7), (8, 9)
REDUCE2, OWN_REDUCE2, PIECE_GATHER, CROSS = 10, 11, 12, 13
DEGREE = (5, 14)
PHASES = 15
CROSS_SLOT = SIDE - 2
SWAP_SLOT = SIDE + 2
PIECE_SLOT = SIDE + 6
SLOTS = SIDE + 9
LOAD_UNITS, LOAD_LABELS, LOAD_MASK, STORE_ROOT, STORE_OWN = range(5)


def spread_kernel(
    mask_hbm,
    emb_hbm,
    lab_hbm,
    parts_hbm,
    root_hbm,
    mask_ref,
    emb_ref,
    uj,
    ui,
    kmat,
    lab,
    sc1,
    sc2,
    part1,
    part2,
    rcv1,
    acc,
    deg,
    root,
    root_wide,
    send_sem,
    recv_sem,
    local_sem,
):
    row = lax.axis_index("row")
    col = lax.axis_index("col")
    y = lax.div(row, 4)
    z_lo = lax.rem(row, 4)
    z_hi = lax.div(col, 8)
    c = lax.rem(col, 8)
    core = lax.rem(col, 2)
    z = z_hi * 4 + z_lo

    def at(new_y, new_z):
        return (new_y * 4 + lax.rem(new_z, 4), lax.div(new_z, 4) * 8 + c)

    def gather_peer(k):
        return at(lax.rem(y + core * k, SIDE), lax.rem(z + (1 - core) * k, SIDE))

    def reduce_peer(k):
        return at(lax.rem(y + (1 - core) * k, SIDE), lax.rem(z + core * k, SIDE))

    def swap_index(k):
        return lax.rem(c + k, SIDE)

    def swap_peer(k):
        return (row, z_hi * 8 + swap_index(k))

    partner_c = c + 1 - 2 * core
    partner = (row, z_hi * 8 + partner_c)

    def beside(position):
        return (position[0], lax.div(position[1], 8) * 8 + partner_c)

    def cross_peer(k):
        return beside(reduce_peer(k))

    def x_peer(k):
        return swap_peer(2 * k)

    own_rows = pl.ds(pl.multiple_of(c * PIECE, PIECE), PIECE)
    own_lanes = pl.ds(pl.multiple_of(c * LANES, LANES), LANES)

    def local(slot, src, dst):
        copy = pltpu.make_async_copy(src, dst, local_sem.at[slot])
        copy.start()
        return copy

    load_units = local(LOAD_UNITS, emb_hbm, emb_ref)
    load_labels = local(LOAD_LABELS, lab_hbm.at[:, own_lanes], lab.at[0, own_rows, :])
    load_mask = local(LOAD_MASK, mask_hbm, mask_ref)
    barrier = pltpu.get_barrier_semaphore()
    for k in FAR_FIRST:
        for peer in (gather_peer(k), beside(gather_peer(k)), swap_peer(k)):
            pl.semaphore_signal(barrier, inc=1, device_id=peer, device_id_type=MESH)

    def describe(phase, src, dst, device, slot=None):
        return pltpu.make_async_remote_copy(
            src_ref=src,
            dst_ref=dst,
            send_sem=send_sem.at[phase],
            recv_sem=recv_sem.at[phase if slot is None else PHASES + slot],
            device_id=device,
            device_id_type=MESH,
        )

    def send(phase, src, dst, device, slot=None):
        copy = describe(phase, src, dst, device, slot)
        copy.start()
        return copy

    sent = []

    def whole(phase, ref):
        copy = describe(phase, ref, ref, partner)
        sent.append(copy)
        return copy

    low, high = slice(0, LANES), slice(LANES, 2 * LANES)
    load_units.wait()
    values = emb_ref[...].astype(jnp.float32)
    norm = lax.rsqrt(jnp.sum(values * values, axis=1, keepdims=True) + EPSILON)
    uj[0, own_rows, :] = (values * norm).astype(jnp.bfloat16)

    pl.semaphore_wait(barrier, 3 * (SIDE - 1))

    own_low = uj.at[0, own_rows, low]
    for k in (2, 1, 3):
        for peer in (x_peer(k), (row, z_hi * 8 + swap_index(2 * k) + 1 - 2 * core)):
            send(UNIT_SWAP, own_low, own_low, peer, slot=SWAP_SLOT + k)
    send(UNIT_SWAP, own_low, own_low, partner, slot=SWAP_SLOT)
    piece = uj.at[0, own_rows, high]
    group_of = {0: 0, 1: 0, 7: 0, 2: 1, 6: 1, 3: 2, 5: 2, 4: 2}
    for k in FAR_FIRST:
        for peer in (gather_peer(k), cross_peer(k)):
            slot = PIECE_SLOT + group_of[k]
            send(PIECE_GATHER, piece, uj.at[k, own_rows, high], peer, slot=slot)
    send(PIECE_GATHER, piece, piece, partner, slot=PIECE_SLOT)
    for k in range(1, SIDE):
        lanes = pl.ds(pl.multiple_of(swap_index(k) * LANES, LANES), LANES)
        send(LABEL_SWAP, lab_hbm.at[:, lanes], lab.at[0, own_rows, :], swap_peer(k))

    others = slice(1, SIDE)
    pair = lax.div(c, 2) * 2 * PIECE

    def pair_rows(k):
        start = lax.rem(pair + (4 - k) * 2 * PIECE, CHUNK)
        return pl.ds(pl.multiple_of(start, 2 * PIECE), 2 * PIECE)

    def gather_pair(x_back):
        count = 1 if x_back == 0 else 2
        region = uj.at[0, 0 : count * PIECE, low]
        describe(UNIT_SWAP, region, region, partner, slot=SWAP_SLOT + x_back).wait_recv()
        rows = pair_rows(x_back)
        for k in FAR_FIRST:
            send(UNIT_GATHER, uj.at[0, rows, low], uj.at[k, rows, low], gather_peer(k), slot=k - 1)

    def cross_group(group, count, slots):
        region = uj.at[0, 0 : count * PIECE, low]
        describe(PIECE_GATHER, region, region, partner, slot=PIECE_SLOT + group).wait_recv()
        for first, last in slots:
            block = uj.at[first:last, pair_rows(0), high]
            for k in (2, 1, 3):
                send(CROSS, block, block, x_peer(k), slot=CROSS_SLOT + k)

    def pass_pair(k):
        block = uj.at[others, pair_rows(k), high]
        send(UNIT_PASS, block, ui.at[others, pair_rows(k), high], partner)

    gather_pair(0)
    gather_pair(1)
    gather_pair(3)
    cross_group(0, 5, ((0, 2), (7, 8)))
    gather_pair(2)
    cross_group(1, 4, ((2, 3), (6, 7)))
    cross_group(2, 6, ((3, 6),))
    whole(UNIT_SWAP, uj.at[0, 0 : (SIDE - 1) * PIECE, low])
    whole(UNIT_GATHER, uj.at[others, :, low])
    whole(PIECE_GATHER, uj.at[0:5, 0 : 3 * PIECE, low])
    whole(CROSS, uj.at[:, 0 : 6 * PIECE, high])
    pass_pair(0)
    load_labels.wait()
    whole(LABEL_SWAP, lab.at[0, 0 : (SIDE - 1) * PIECE, :]).wait_recv()
    for k in FAR_FIRST:
        send(LABEL_GATHER, lab.at[0], lab.at[k], gather_peer(k))
    for k in NEAR_FIRST:
        describe(UNIT_GATHER, uj.at[k, :, low], uj.at[k, :, low], partner, slot=k - 1).wait_recv()
        send(UNIT_PASS, uj.at[k, :, low], ui.at[k, :, low], partner)
    for k in (1, 3, 2):
        block = uj.at[:, pair_rows(k), high]
        describe(CROSS, block, block, partner, slot=CROSS_SLOT + k).wait_recv()
        pass_pair(k)
    scale = SHARPNESS * math.sqrt(emb_ref.shape[1]) * math.log2(math.e)
    lane = lax.broadcasted_iota(jnp.int32, (1, 2 * CHUNK), 1)

    def block_of(chunk_y, chunk_z):
        return chunk_y * 4 + lax.rem(chunk_z, 4)

    def back(position, k):
        return lax.rem(position + SIDE - k, SIDE)

    def kept(row_block, col_block):
        low = jnp.minimum(row_block, col_block)
        high = jnp.maximum(row_block, col_block)
        return jnp.where(row_block == col_block, 1, mask_ref[low, high]).astype(jnp.float32)

    col_blocks = [block_of(back(y, core * k), back(z, (1 - core) * k)) for k in range(SIDE)]
    row_blocks = [block_of(back(y, (1 - core) * k), back(z, core * k)) for k in range(SIDE)]

    def kept_lanes(k, quad):
        bits = [kept(row_blocks[k], col_blocks[4 * quad + j]) for j in range(4)]
        return jnp.where(
            lane < 2 * HALF,
            jnp.where(lane < HALF, bits[0], bits[1]),
            jnp.where(lane < 3 * HALF, bits[2], bits[3]),
        )

    def make_tile(vecs, k, half, quad, keep):
        cosine = lax.dot_general(
            vecs[k],
            uj[4 * quad : 4 * quad + 4, half * HALF : (half + 1) * HALF, :].reshape(
                4 * HALF, emb_ref.shape[1]
            ),
            (((1,), (1,)), ((), ())),
            preferred_element_type=jnp.float32,
        )
        weights = jnp.exp2(cosine * scale)
        if k == 0 and quad == 0:
            own_row = lax.broadcasted_iota(jnp.int32, weights.shape, 0)
            own_col = lax.broadcasted_iota(jnp.int32, weights.shape, 1)
            own = (own_col < HALF) & (own_row == own_col + half * HALF)
            weights = jnp.where(own, 0.0, weights)
        start = (2 * half + quad) * 4 * HALF
        kmat[k, :, start : start + 4 * HALF] = weights.astype(jnp.bfloat16) * keep.astype(
            jnp.bfloat16
        )
        return jnp.sum(weights, axis=0, keepdims=True) * keep

    load_mask.wait()
    sums = {}
    for quad in range(2):
        keep = kept_lanes(0, quad)
        for half in range(2):
            sums[half, quad] = make_tile(uj, 0, half, quad, keep)
    whole(UNIT_PASS, ui.at[others]).wait_recv()
    keeps = [[kept_lanes(k, quad) for k in range(SIDE)] for quad in range(2)]
    for half in range(2):
        for quad in range(2):
            total = sums[half, quad]
            for k in range(1, SIDE):
                total = total + make_tile(ui, k, half, quad, keeps[quad][k])
            for j in range(4):
                degrees = total[:, j * HALF : (j + 1) * HALF]
                deg[half, 0, 4 * quad + j : 4 * quad + j + 1, :] = jnp.concatenate(
                    [degrees, degrees], axis=1
                )
        for k in FAR_FIRST:
            send(DEGREE[half], deg.at[half, 0], deg.at[half, k], gather_peer(k))
    whole(LABEL_GATHER, lab.at[others]).wait_recv()
    seeds = lab[0].astype(jnp.float32)

    def scale_half(half):
        whole(DEGREE[half], deg.at[half, others]).wait_recv()
        degree = deg[half, 0]
        for k in range(1, SIDE):
            degree = degree + pltpu.roll(deg[half, k], k, 0)
        inv_root = jnp.transpose(lax.rsqrt(degree))[:HALF]
        for k in range(SIDE):
            values = lab[k, half * HALF : (half + 1) * HALF, :].astype(jnp.float32)
            sc1[half, k] = (values * inv_root[:, k : k + 1]).astype(jnp.bfloat16)
        return inv_root[:, 0:1]

    def rows_of(half):
        return pl.ds(half * HALF, HALF)

    def product(rows, lanes, scaled):
        matrix = kmat[:, rows, lanes]
        return jnp.dot(
            matrix.reshape(-1, matrix.shape[2]),
            scaled.reshape(-1, LANES),
            preferred_element_type=jnp.float32,
        ).reshape(SIDE, -1, LANES)

    first_half, last_half = slice(0, SIDE * HALF), slice(SIDE * HALF, SIDE * CHUNK)
    own_roots = [scale_half(0)]
    acc[...] = product(slice(None), first_half, sc1[0])
    own_roots.append(scale_half(1))
    spreads = []
    for half in range(2):
        rows = rows_of(half)
        spread = acc[:, rows, :] + product(rows, last_half, sc1[1])
        spreads.append(spread[0])
        part1[:, rows, :] = spread.astype(jnp.bfloat16)
        for k in FAR_FIRST:
            send(REDUCE1[half], part1.at[k, rows, :], rcv1.at[k, rows, :], reduce_peer(SIDE - k))
    own_root = jnp.concatenate(own_roots, axis=0)
    root[...] = jnp.broadcast_to(own_root, root.shape)
    for half in range(2):
        rows = rows_of(half)
        picked = slice(half * HALF, (half + 1) * HALF)
        whole(REDUCE1[half], rcv1.at[others, rows, :]).wait_recv()
        total = spreads[half]
        for k in range(1, SIDE):
            total = total + rcv1[k, rows, :].astype(jnp.float32)
        current = MIXING * own_root[picked] * total + (1.0 - MIXING) * seeds[picked]
        sc2[half, 0] = (own_root[picked] * current).astype(jnp.bfloat16)
        for k in FAR_FIRST:
            send(GATHER2[half], sc2.at[half, 0], sc2.at[half, k], gather_peer(k))
    root_wide[...] = jnp.concatenate([root[own_rows, :]] * SIDE, axis=1)
    store_root = local(STORE_ROOT, root_wide, root_hbm)
    whole(GATHER2[0], sc2.at[0, others]).wait_recv()
    acc[...] = product(slice(None), first_half, sc2[0])
    whole(GATHER2[1], sc2.at[1, others]).wait_recv()
    for half in range(2):
        rows = rows_of(half)
        spread = acc[:, rows, :] + product(rows, last_half, sc2[1])
        part2[:, rows, :] = spread.astype(jnp.bfloat16)
        for k in FAR_FIRST:
            new_row, new_col = reduce_peer(SIDE - k)
            first = lax.div(new_col, SIDE) * SIDE
            for member in range(half * SIDE // 2, (half + 1) * SIDE // 2):
                send(
                    REDUCE2,
                    part2.at[k, member * PIECE : (member + 1) * PIECE, :],
                    parts_hbm.at[k, :, own_lanes],
                    (new_row, first + member),
                )
    for k in range(1, SIDE):
        rows = pl.ds(pl.multiple_of(swap_index(k) * PIECE, PIECE), PIECE)
        send(OWN_REDUCE2, part2.at[0, rows, :], parts_hbm.at[0, :, own_lanes], swap_peer(k))
    store_own = local(STORE_OWN, part2.at[0, own_rows, :], parts_hbm.at[0, :, own_lanes])
    store_root.wait()
    store_own.wait()
    whole(OWN_REDUCE2, rcv1.at[0, 0 : (SIDE - 1) * PIECE, :]).wait_recv()
    whole(REDUCE2, rcv1.at[others]).wait_recv()
    for copy in sent:
        copy.wait_send()


def shards(embeddings, labels, tile_mask):
    width = embeddings.shape[1]
    anywhere = pl.BlockSpec(memory_space=pl.ANY)
    units = pltpu.VMEM((SIDE, CHUNK, width), jnp.bfloat16)
    chunks = pltpu.VMEM((SIDE, CHUNK, LANES), jnp.bfloat16)
    parts, root = pl.pallas_call(
        spread_kernel,
        out_shape=(
            jax.ShapeDtypeStruct((SIDE, *labels.shape), jnp.bfloat16),
            jax.ShapeDtypeStruct(labels.shape, jnp.float32),
        ),
        in_specs=[anywhere] * 3,
        out_specs=(anywhere, anywhere),
        scratch_shapes=[
            pltpu.SMEM(tile_mask.shape, jnp.int32),
            pltpu.VMEM(embeddings.shape, jnp.bfloat16),
            units,
            units,
            pltpu.VMEM((SIDE, CHUNK, SIDE * CHUNK), jnp.bfloat16),
            chunks,
            pltpu.VMEM((2, SIDE, HALF, LANES), jnp.bfloat16),
            pltpu.VMEM((2, SIDE, HALF, LANES), jnp.bfloat16),
            chunks,
            chunks,
            chunks,
            pltpu.VMEM((SIDE, CHUNK, LANES), jnp.float32),
            pltpu.VMEM((2, SIDE, SIDE, CHUNK), jnp.float32),
            pltpu.VMEM((CHUNK, LANES), jnp.float32),
            pltpu.VMEM(labels.shape, jnp.float32),
            pltpu.SemaphoreType.DMA((PHASES,)),
            pltpu.SemaphoreType.DMA((PHASES + SLOTS,)),
            pltpu.SemaphoreType.DMA((5,)),
        ],
        compiler_params=pltpu.CompilerParams(collective_id=0, has_side_effects=True),
    )(tile_mask, embeddings, labels)
    spread = parts[0].astype(jnp.float32)
    for k in range(1, SIDE):
        spread = spread + parts[k].astype(jnp.float32)
    current = MIXING * root * spread + (1.0 - MIXING) * labels.astype(jnp.float32)
    return current.astype(jnp.bfloat16)


def solution(mesh):
    placed = (P(("row", "col"), None), P(("row", "col"), None), P())
    return jax.shard_map(
        shards, mesh=mesh, in_specs=placed, out_specs=P(("row", "col"), None), check_vma=False
    )
```

```python
import math

import jax
import jax.numpy as jnp
from jax import lax
from jax.experimental import pallas as pl
from jax.experimental.pallas import tpu as pltpu
from jax.sharding import PartitionSpec as P

MIXING = 0.9
SHARPNESS = 3.0
EPSILON = 1e-06

SIDE = 8
CHUNK = 128
PIECE = 16
LANES = 128
MESH = pl.DeviceIdType.MESH
FAR_FIRST = (4, 3, 5, 2, 6, 1, 7)
NEAR_FIRST = (1, 7, 2, 6, 3, 5, 4)

HALF = CHUNK // 2
UNIT_SWAP, LABEL_SWAP, UNIT_GATHER, UNIT_PASS, LABEL_GATHER = range(5)
REDUCE1, GATHER2 = (6, 7, 15, 16), (8, 9)
REDUCE2, OWN_REDUCE2, PIECE_GATHER, CROSS = 10, 11, 12, 13
DEGREE = (5, 14)
PHASES = 17
QUARTER = HALF // 2
CROSS_SLOT = SIDE - 2
SWAP_SLOT = SIDE + 2
PIECE_SLOT = SIDE + 6
SLOTS = SIDE + 9
LOAD_UNITS, LOAD_LABELS, LOAD_MASK, STORE_ROOT, STORE_OWN = range(5)


def spread_kernel(
    mask_hbm,
    emb_hbm,
    lab_hbm,
    parts_hbm,
    root_hbm,
    mask_ref,
    emb_ref,
    uj,
    ui,
    kmat,
    lab,
    sc1,
    sc2,
    part1,
    part2,
    rcv1,
    acc,
    deg,
    root,
    root_wide,
    send_sem,
    recv_sem,
    local_sem,
):
    row = lax.axis_index("row")
    col = lax.axis_index("col")
    y = lax.div(row, 4)
    z_lo = lax.rem(row, 4)
    z_hi = lax.div(col, 8)
    c = lax.rem(col, 8)
    core = lax.rem(col, 2)
    z = z_hi * 4 + z_lo

    def at(new_y, new_z):
        return (new_y * 4 + lax.rem(new_z, 4), lax.div(new_z, 4) * 8 + c)

    def gather_peer(k):
        return at(lax.rem(y + core * k, SIDE), lax.rem(z + (1 - core) * k, SIDE))

    def reduce_peer(k):
        return at(lax.rem(y + (1 - core) * k, SIDE), lax.rem(z + core * k, SIDE))

    def swap_index(k):
        return lax.rem(c + k, SIDE)

    def swap_peer(k):
        return (row, z_hi * 8 + swap_index(k))

    partner_c = c + 1 - 2 * core
    partner = (row, z_hi * 8 + partner_c)

    def beside(position):
        return (position[0], lax.div(position[1], 8) * 8 + partner_c)

    def cross_peer(k):
        return beside(reduce_peer(k))

    def x_peer(k):
        return swap_peer(2 * k)

    own_rows = pl.ds(pl.multiple_of(c * PIECE, PIECE), PIECE)
    own_lanes = pl.ds(pl.multiple_of(c * LANES, LANES), LANES)

    def local(slot, src, dst):
        copy = pltpu.make_async_copy(src, dst, local_sem.at[slot])
        copy.start()
        return copy

    load_units = local(LOAD_UNITS, emb_hbm, emb_ref)
    load_labels = local(LOAD_LABELS, lab_hbm.at[:, own_lanes], lab.at[0, own_rows, :])
    load_mask = local(LOAD_MASK, mask_hbm, mask_ref)
    barrier = pltpu.get_barrier_semaphore()
    for k in FAR_FIRST:
        for peer in (gather_peer(k), beside(gather_peer(k)), swap_peer(k)):
            pl.semaphore_signal(barrier, inc=1, device_id=peer, device_id_type=MESH)

    def describe(phase, src, dst, device, slot=None):
        return pltpu.make_async_remote_copy(
            src_ref=src,
            dst_ref=dst,
            send_sem=send_sem.at[phase],
            recv_sem=recv_sem.at[phase if slot is None else PHASES + slot],
            device_id=device,
            device_id_type=MESH,
        )

    def send(phase, src, dst, device, slot=None):
        copy = describe(phase, src, dst, device, slot)
        copy.start()
        return copy

    sent = []

    def whole(phase, ref):
        copy = describe(phase, ref, ref, partner)
        sent.append(copy)
        return copy

    low, high = slice(0, LANES), slice(LANES, 2 * LANES)
    load_units.wait()
    values = emb_ref[...].astype(jnp.float32)
    norm = lax.rsqrt(jnp.sum(values * values, axis=1, keepdims=True) + EPSILON)
    uj[0, own_rows, :] = (values * norm).astype(jnp.bfloat16)

    pl.semaphore_wait(barrier, 3 * (SIDE - 1))

    own_low = uj.at[0, own_rows, low]
    for k in (2, 1, 3):
        for peer in (x_peer(k), (row, z_hi * 8 + swap_index(2 * k) + 1 - 2 * core)):
            send(UNIT_SWAP, own_low, own_low, peer, slot=SWAP_SLOT + k)
    send(UNIT_SWAP, own_low, own_low, partner, slot=SWAP_SLOT)
    piece = uj.at[0, own_rows, high]
    group_of = {0: 0, 1: 0, 7: 0, 2: 1, 6: 1, 3: 2, 5: 2, 4: 2}
    for k in FAR_FIRST:
        for peer in (gather_peer(k), cross_peer(k)):
            slot = PIECE_SLOT + group_of[k]
            send(PIECE_GATHER, piece, uj.at[k, own_rows, high], peer, slot=slot)
    send(PIECE_GATHER, piece, piece, partner, slot=PIECE_SLOT)
    for k in range(1, SIDE):
        lanes = pl.ds(pl.multiple_of(swap_index(k) * LANES, LANES), LANES)
        send(LABEL_SWAP, lab_hbm.at[:, lanes], lab.at[0, own_rows, :], swap_peer(k))

    others = slice(1, SIDE)
    pair = lax.div(c, 2) * 2 * PIECE

    def pair_rows(k):
        start = lax.rem(pair + (4 - k) * 2 * PIECE, CHUNK)
        return pl.ds(pl.multiple_of(start, 2 * PIECE), 2 * PIECE)

    def gather_pair(x_back):
        count = 1 if x_back == 0 else 2
        region = uj.at[0, 0 : count * PIECE, low]
        describe(UNIT_SWAP, region, region, partner, slot=SWAP_SLOT + x_back).wait_recv()
        rows = pair_rows(x_back)
        for k in FAR_FIRST:
            send(UNIT_GATHER, uj.at[0, rows, low], uj.at[k, rows, low], gather_peer(k), slot=k - 1)

    def cross_group(group, count, slots):
        region = uj.at[0, 0 : count * PIECE, low]
        describe(PIECE_GATHER, region, region, partner, slot=PIECE_SLOT + group).wait_recv()
        for first, last in slots:
            block = uj.at[first:last, pair_rows(0), high]
            for k in (2, 1, 3):
                send(CROSS, block, block, x_peer(k), slot=CROSS_SLOT + k)

    def pass_pair(k):
        block = uj.at[others, pair_rows(k), high]
        send(UNIT_PASS, block, ui.at[others, pair_rows(k), high], partner)

    gather_pair(0)
    gather_pair(1)
    gather_pair(3)
    cross_group(0, 5, ((0, 2), (7, 8)))
    gather_pair(2)
    cross_group(1, 4, ((2, 3), (6, 7)))
    cross_group(2, 6, ((3, 6),))
    whole(UNIT_SWAP, uj.at[0, 0 : (SIDE - 1) * PIECE, low])
    whole(UNIT_GATHER, uj.at[others, :, low])
    whole(PIECE_GATHER, uj.at[0:5, 0 : 3 * PIECE, low])
    whole(CROSS, uj.at[:, 0 : 6 * PIECE, high])
    pass_pair(0)
    load_labels.wait()
    whole(LABEL_SWAP, lab.at[0, 0 : (SIDE - 1) * PIECE, :]).wait_recv()
    for k in FAR_FIRST:
        send(LABEL_GATHER, lab.at[0], lab.at[k], gather_peer(k))
    for k in NEAR_FIRST:
        describe(UNIT_GATHER, uj.at[k, :, low], uj.at[k, :, low], partner, slot=k - 1).wait_recv()
        send(UNIT_PASS, uj.at[k, :, low], ui.at[k, :, low], partner)
    for k in (1, 3, 2):
        block = uj.at[:, pair_rows(k), high]
        describe(CROSS, block, block, partner, slot=CROSS_SLOT + k).wait_recv()
        pass_pair(k)
    scale = SHARPNESS * math.sqrt(emb_ref.shape[1]) * math.log2(math.e)
    lane = lax.broadcasted_iota(jnp.int32, (1, 2 * CHUNK), 1)

    def block_of(chunk_y, chunk_z):
        return chunk_y * 4 + lax.rem(chunk_z, 4)

    def back(position, k):
        return lax.rem(position + SIDE - k, SIDE)

    def kept(row_block, col_block):
        low = jnp.minimum(row_block, col_block)
        high = jnp.maximum(row_block, col_block)
        return jnp.where(row_block == col_block, 1, mask_ref[low, high]).astype(jnp.float32)

    col_blocks = [block_of(back(y, core * k), back(z, (1 - core) * k)) for k in range(SIDE)]
    row_blocks = [block_of(back(y, (1 - core) * k), back(z, core * k)) for k in range(SIDE)]

    def kept_lanes(k, quad):
        bits = [kept(row_blocks[k], col_blocks[4 * quad + j]) for j in range(4)]
        return jnp.where(
            lane < 2 * HALF,
            jnp.where(lane < HALF, bits[0], bits[1]),
            jnp.where(lane < 3 * HALF, bits[2], bits[3]),
        )

    def make_tile(vecs, k, half, quad, keep):
        cosine = lax.dot_general(
            vecs[k],
            uj[4 * quad : 4 * quad + 4, half * HALF : (half + 1) * HALF, :].reshape(
                4 * HALF, emb_ref.shape[1]
            ),
            (((1,), (1,)), ((), ())),
            preferred_element_type=jnp.float32,
        )
        weights = jnp.exp2(cosine * scale)
        if k == 0 and quad == 0:
            own_row = lax.broadcasted_iota(jnp.int32, weights.shape, 0)
            own_col = lax.broadcasted_iota(jnp.int32, weights.shape, 1)
            own = (own_col < HALF) & (own_row == own_col + half * HALF)
            weights = jnp.where(own, 0.0, weights)
        start = (2 * half + quad) * 4 * HALF
        kmat[k, :, start : start + 4 * HALF] = weights.astype(jnp.bfloat16) * keep.astype(
            jnp.bfloat16
        )
        return jnp.sum(weights, axis=0, keepdims=True) * keep

    load_mask.wait()
    sums = {}
    for quad in range(2):
        keep = kept_lanes(0, quad)
        for half in range(2):
            sums[half, quad] = make_tile(uj, 0, half, quad, keep)
    whole(UNIT_PASS, ui.at[others]).wait_recv()
    keeps = [[kept_lanes(k, quad) for k in range(SIDE)] for quad in range(2)]
    for half in range(2):
        for quad in range(2):
            total = sums[half, quad]
            for k in range(1, SIDE):
                total = total + make_tile(ui, k, half, quad, keeps[quad][k])
            for j in range(4):
                degrees = total[:, j * HALF : (j + 1) * HALF]
                deg[half, 0, 4 * quad + j : 4 * quad + j + 1, :] = jnp.concatenate(
                    [degrees, degrees], axis=1
                )
        for k in FAR_FIRST:
            send(DEGREE[half], deg.at[half, 0], deg.at[half, k], gather_peer(k))
    whole(LABEL_GATHER, lab.at[others]).wait_recv()
    seeds = lab[0].astype(jnp.float32)

    def scale_half(half):
        whole(DEGREE[half], deg.at[half, others]).wait_recv()
        degree = deg[half, 0]
        for k in range(1, SIDE):
            degree = degree + pltpu.roll(deg[half, k], k, 0)
        inv_root = jnp.transpose(lax.rsqrt(degree))[:HALF]
        for k in range(SIDE):
            values = lab[k, half * HALF : (half + 1) * HALF, :].astype(jnp.float32)
            sc1[half, k] = (values * inv_root[:, k : k + 1]).astype(jnp.bfloat16)
        return inv_root[:, 0:1]

    def rows_of(half):
        return pl.ds(half * HALF, HALF)

    def product(rows, lanes, scaled):
        matrix = kmat[:, rows, lanes]
        return jnp.dot(
            matrix.reshape(-1, matrix.shape[2]),
            scaled.reshape(-1, LANES),
            preferred_element_type=jnp.float32,
        ).reshape(SIDE, -1, LANES)

    first_half, last_half = slice(0, SIDE * HALF), slice(SIDE * HALF, SIDE * CHUNK)
    own_roots = [scale_half(0)]
    acc[...] = product(slice(None), first_half, sc1[0])
    own_roots.append(scale_half(1))
    spreads = []
    for half in range(2):
        rows = rows_of(half)
        spread = acc[:, rows, :] + product(rows, last_half, sc1[1])
        spreads.append(spread[0])
        part1[:, rows, :] = spread.astype(jnp.bfloat16)
        for quarter in (2 * half, 2 * half + 1):
            rows = pl.ds(quarter * QUARTER, QUARTER)
            for k in FAR_FIRST:
                part = part1.at[k, rows, :]
                send(REDUCE1[quarter], part, rcv1.at[k, rows, :], reduce_peer(SIDE - k))
    own_root = jnp.concatenate(own_roots, axis=0)
    root[...] = jnp.broadcast_to(own_root, root.shape)
    for quarter in range(4):
        half, inner = quarter // 2, quarter % 2 * QUARTER
        rows = pl.ds(quarter * QUARTER, QUARTER)
        picked = slice(quarter * QUARTER, (quarter + 1) * QUARTER)
        whole(REDUCE1[quarter], rcv1.at[others, rows, :]).wait_recv()
        total = spreads[half][inner : inner + QUARTER]
        for k in range(1, SIDE):
            total = total + rcv1[k, rows, :].astype(jnp.float32)
        current = MIXING * own_root[picked] * total + (1.0 - MIXING) * seeds[picked]
        rows = pl.ds(inner, QUARTER)
        sc2[half, 0, rows, :] = (own_root[picked] * current).astype(jnp.bfloat16)
        for k in FAR_FIRST:
            send(GATHER2[half], sc2.at[half, 0, rows, :], sc2.at[half, k, rows, :], gather_peer(k))
    root_wide[...] = jnp.concatenate([root[own_rows, :]] * SIDE, axis=1)
    store_root = local(STORE_ROOT, root_wide, root_hbm)
    whole(GATHER2[0], sc2.at[0, others]).wait_recv()
    acc[...] = product(slice(None), first_half, sc2[0])
    whole(GATHER2[1], sc2.at[1, others]).wait_recv()
    for half in range(2):
        rows = rows_of(half)
        spread = acc[:, rows, :] + product(rows, last_half, sc2[1])
        part2[:, rows, :] = spread.astype(jnp.bfloat16)
        for k in FAR_FIRST:
            new_row, new_col = reduce_peer(SIDE - k)
            first = lax.div(new_col, SIDE) * SIDE
            for member in range(half * SIDE // 2, (half + 1) * SIDE // 2):
                send(
                    REDUCE2,
                    part2.at[k, member * PIECE : (member + 1) * PIECE, :],
                    parts_hbm.at[k, :, own_lanes],
                    (new_row, first + member),
                )
    for k in range(1, SIDE):
        rows = pl.ds(pl.multiple_of(swap_index(k) * PIECE, PIECE), PIECE)
        send(OWN_REDUCE2, part2.at[0, rows, :], parts_hbm.at[0, :, own_lanes], swap_peer(k))
    store_own = local(STORE_OWN, part2.at[0, own_rows, :], parts_hbm.at[0, :, own_lanes])
    store_root.wait()
    store_own.wait()
    whole(OWN_REDUCE2, rcv1.at[0, 0 : (SIDE - 1) * PIECE, :]).wait_recv()
    whole(REDUCE2, rcv1.at[others]).wait_recv()
    for copy in sent:
        copy.wait_send()


def shards(embeddings, labels, tile_mask):
    width = embeddings.shape[1]
    anywhere = pl.BlockSpec(memory_space=pl.ANY)
    units = pltpu.VMEM((SIDE, CHUNK, width), jnp.bfloat16)
    chunks = pltpu.VMEM((SIDE, CHUNK, LANES), jnp.bfloat16)
    parts, root = pl.pallas_call(
        spread_kernel,
        out_shape=(
            jax.ShapeDtypeStruct((SIDE, *labels.shape), jnp.bfloat16),
            jax.ShapeDtypeStruct(labels.shape, jnp.float32),
        ),
        in_specs=[anywhere] * 3,
        out_specs=(anywhere, anywhere),
        scratch_shapes=[
            pltpu.SMEM(tile_mask.shape, jnp.int32),
            pltpu.VMEM(embeddings.shape, jnp.bfloat16),
            units,
            units,
            pltpu.VMEM((SIDE, CHUNK, SIDE * CHUNK), jnp.bfloat16),
            chunks,
            pltpu.VMEM((2, SIDE, HALF, LANES), jnp.bfloat16),
            pltpu.VMEM((2, SIDE, HALF, LANES), jnp.bfloat16),
            chunks,
            chunks,
            chunks,
            pltpu.VMEM((SIDE, CHUNK, LANES), jnp.float32),
            pltpu.VMEM((2, SIDE, SIDE, CHUNK), jnp.float32),
            pltpu.VMEM((CHUNK, LANES), jnp.float32),
            pltpu.VMEM(labels.shape, jnp.float32),
            pltpu.SemaphoreType.DMA((PHASES,)),
            pltpu.SemaphoreType.DMA((PHASES + SLOTS,)),
            pltpu.SemaphoreType.DMA((5,)),
        ],
        compiler_params=pltpu.CompilerParams(collective_id=0, has_side_effects=True),
    )(tile_mask, embeddings, labels)
    spread = parts[0].astype(jnp.float32)
    for k in range(1, SIDE):
        spread = spread + parts[k].astype(jnp.float32)
    current = MIXING * root * spread + (1.0 - MIXING) * labels.astype(jnp.float32)
    return current.astype(jnp.bfloat16)


def solution(mesh):
    placed = (P(("row", "col"), None), P(("row", "col"), None), P())
    return jax.shard_map(
        shards, mesh=mesh, in_specs=placed, out_specs=P(("row", "col"), None), check_vma=False
    )
```

```python
import math

import jax
import jax.numpy as jnp
from jax import lax
from jax.experimental import pallas as pl
from jax.experimental.pallas import tpu as pltpu
from jax.sharding import PartitionSpec as P

MIXING = 0.9
SHARPNESS = 3.0
EPSILON = 1e-06

SIDE = 8
CHUNK = 128
PIECE = 16
LANES = 128
MESH = pl.DeviceIdType.MESH
FAR_FIRST = (4, 3, 5, 2, 6, 1, 7)
NEAR_FIRST = (1, 7, 2, 6, 3, 5, 4)

HALF = CHUNK // 2
UNIT_SWAP, LABEL_SWAP, UNIT_GATHER, UNIT_PASS, LABEL_GATHER = range(5)
REDUCE1, GATHER2 = (6, 7), (8, 9)
REDUCE2, OWN_REDUCE2, PIECE_GATHER, CROSS = 10, 11, 12, 13
DEGREE = (5, 14)
PHASES = 15
CROSS_SLOT = SIDE - 2
SWAP_SLOT = SIDE + 2
PIECE_SLOT = SIDE + 6
SLOTS = SIDE + 9
LOAD_UNITS, LOAD_LABELS, LOAD_MASK, STORE_ROOT, STORE_OWN = range(5)


def spread_kernel(
    mask_hbm,
    emb_hbm,
    lab_hbm,
    parts_hbm,
    root_hbm,
    mask_ref,
    emb_ref,
    uj,
    ui,
    kmat,
    lab,
    sc1,
    sc2,
    part1,
    part2,
    rcv1,
    acc,
    deg,
    root,
    root_wide,
    send_sem,
    recv_sem,
    local_sem,
):
    row = lax.axis_index("row")
    col = lax.axis_index("col")
    y = lax.div(row, 4)
    z_lo = lax.rem(row, 4)
    z_hi = lax.div(col, 8)
    c = lax.rem(col, 8)
    core = lax.rem(col, 2)
    z = z_hi * 4 + z_lo

    def at(new_y, new_z):
        return (new_y * 4 + lax.rem(new_z, 4), lax.div(new_z, 4) * 8 + c)

    def gather_peer(k):
        return at(lax.rem(y + core * k, SIDE), lax.rem(z + (1 - core) * k, SIDE))

    def reduce_peer(k):
        return at(lax.rem(y + (1 - core) * k, SIDE), lax.rem(z + core * k, SIDE))

    def swap_index(k):
        return lax.rem(c + k, SIDE)

    def swap_peer(k):
        return (row, z_hi * 8 + swap_index(k))

    partner_c = c + 1 - 2 * core
    partner = (row, z_hi * 8 + partner_c)

    def beside(position):
        return (position[0], lax.div(position[1], 8) * 8 + partner_c)

    def cross_peer(k):
        return beside(reduce_peer(k))

    def x_peer(k):
        return swap_peer(2 * k)

    own_rows = pl.ds(pl.multiple_of(c * PIECE, PIECE), PIECE)
    own_lanes = pl.ds(pl.multiple_of(c * LANES, LANES), LANES)

    def local(slot, src, dst):
        copy = pltpu.make_async_copy(src, dst, local_sem.at[slot])
        copy.start()
        return copy

    load_units = local(LOAD_UNITS, emb_hbm, emb_ref)
    load_labels = local(LOAD_LABELS, lab_hbm.at[:, own_lanes], lab.at[0, own_rows, :])
    load_mask = local(LOAD_MASK, mask_hbm, mask_ref)
    barrier = pltpu.get_barrier_semaphore()
    for k in FAR_FIRST:
        for peer in (gather_peer(k), beside(gather_peer(k)), swap_peer(k)):
            pl.semaphore_signal(barrier, inc=1, device_id=peer, device_id_type=MESH)

    def describe(phase, src, dst, device, slot=None):
        return pltpu.make_async_remote_copy(
            src_ref=src,
            dst_ref=dst,
            send_sem=send_sem.at[phase],
            recv_sem=recv_sem.at[phase if slot is None else PHASES + slot],
            device_id=device,
            device_id_type=MESH,
        )

    def send(phase, src, dst, device, slot=None):
        copy = describe(phase, src, dst, device, slot)
        copy.start()
        return copy

    sent = []

    def whole(phase, ref):
        copy = describe(phase, ref, ref, partner)
        sent.append(copy)
        return copy

    low, high = slice(0, LANES), slice(LANES, 2 * LANES)
    load_units.wait()
    values = emb_ref[...].astype(jnp.float32)
    norm = lax.rsqrt(jnp.sum(values * values, axis=1, keepdims=True) + EPSILON)
    uj[0, own_rows, :] = (values * norm).astype(jnp.bfloat16)

    pl.semaphore_wait(barrier, 3 * (SIDE - 1))

    own_low = uj.at[0, own_rows, low]
    for k in (2, 1, 3):
        for peer in (x_peer(k), (row, z_hi * 8 + swap_index(2 * k) + 1 - 2 * core)):
            send(UNIT_SWAP, own_low, own_low, peer, slot=SWAP_SLOT + k)
    send(UNIT_SWAP, own_low, own_low, partner, slot=SWAP_SLOT)
    piece = uj.at[0, own_rows, high]
    group_of = {0: 0, 1: 0, 7: 0, 2: 1, 6: 1, 3: 1, 5: 1, 4: 1}
    for k in FAR_FIRST:
        for peer in (gather_peer(k), cross_peer(k)):
            slot = PIECE_SLOT + group_of[k]
            send(PIECE_GATHER, piece, uj.at[k, own_rows, high], peer, slot=slot)
    send(PIECE_GATHER, piece, piece, partner, slot=PIECE_SLOT)
    for k in range(1, SIDE):
        lanes = pl.ds(pl.multiple_of(swap_index(k) * LANES, LANES), LANES)
        send(LABEL_SWAP, lab_hbm.at[:, lanes], lab.at[0, own_rows, :], swap_peer(k))

    others = slice(1, SIDE)
    pair = lax.div(c, 2) * 2 * PIECE

    def pair_rows(k):
        start = lax.rem(pair + (4 - k) * 2 * PIECE, CHUNK)
        return pl.ds(pl.multiple_of(start, 2 * PIECE), 2 * PIECE)

    def gather_pair(x_back):
        count = 1 if x_back == 0 else 2
        region = uj.at[0, 0 : count * PIECE, low]
        describe(UNIT_SWAP, region, region, partner, slot=SWAP_SLOT + x_back).wait_recv()
        rows = pair_rows(x_back)
        for k in FAR_FIRST:
            send(UNIT_GATHER, uj.at[0, rows, low], uj.at[k, rows, low], gather_peer(k), slot=k - 1)

    def cross_group(group, count, slots):
        region = uj.at[0 : count // 5, 0 : 5 * PIECE, low]
        describe(PIECE_GATHER, region, region, partner, slot=PIECE_SLOT + group).wait_recv()
        for first, last in slots:
            block = uj.at[first:last, pair_rows(0), high]
            for k in (2, 1, 3):
                send(CROSS, block, block, x_peer(k), slot=CROSS_SLOT + k)

    def pass_pair(k):
        block = uj.at[others, pair_rows(k), high]
        send(UNIT_PASS, block, ui.at[others, pair_rows(k), high], partner)

    gather_pair(0)
    gather_pair(1)
    gather_pair(3)
    cross_group(0, 5, ((0, 2), (7, 8)))
    gather_pair(2)
    cross_group(1, 10, ((2, 7),))
    whole(UNIT_SWAP, uj.at[0, 0 : (SIDE - 1) * PIECE, low])
    whole(UNIT_GATHER, uj.at[others, :, low])
    whole(PIECE_GATHER, uj.at[0:5, 0 : 3 * PIECE, low])
    whole(CROSS, uj.at[:, 0 : 6 * PIECE, high])
    pass_pair(0)
    load_labels.wait()
    whole(LABEL_SWAP, lab.at[0, 0 : (SIDE - 1) * PIECE, :]).wait_recv()
    for k in FAR_FIRST:
        send(LABEL_GATHER, lab.at[0], lab.at[k], gather_peer(k))
    for k in NEAR_FIRST:
        describe(UNIT_GATHER, uj.at[k, :, low], uj.at[k, :, low], partner, slot=k - 1).wait_recv()
        send(UNIT_PASS, uj.at[k, :, low], ui.at[k, :, low], partner)
    for k in (1, 3, 2):
        block = uj.at[:, pair_rows(k), high]
        describe(CROSS, block, block, partner, slot=CROSS_SLOT + k).wait_recv()
        pass_pair(k)
    scale = SHARPNESS * math.sqrt(emb_ref.shape[1]) * math.log2(math.e)
    lane = lax.broadcasted_iota(jnp.int32, (1, 2 * CHUNK), 1)

    def block_of(chunk_y, chunk_z):
        return chunk_y * 4 + lax.rem(chunk_z, 4)

    def back(position, k):
        return lax.rem(position + SIDE - k, SIDE)

    def kept(row_block, col_block):
        low = jnp.minimum(row_block, col_block)
        high = jnp.maximum(row_block, col_block)
        return jnp.where(row_block == col_block, 1, mask_ref[low, high]).astype(jnp.float32)

    col_blocks = [block_of(back(y, core * k), back(z, (1 - core) * k)) for k in range(SIDE)]
    row_blocks = [block_of(back(y, (1 - core) * k), back(z, core * k)) for k in range(SIDE)]

    def kept_lanes(k, quad):
        bits = [kept(row_blocks[k], col_blocks[4 * quad + j]) for j in range(4)]
        return jnp.where(
            lane < 2 * HALF,
            jnp.where(lane < HALF, bits[0], bits[1]),
            jnp.where(lane < 3 * HALF, bits[2], bits[3]),
        )

    def make_tile(vecs, k, half, quad, keep):
        cosine = lax.dot_general(
            vecs[k],
            uj[4 * quad : 4 * quad + 4, half * HALF : (half + 1) * HALF, :].reshape(
                4 * HALF, emb_ref.shape[1]
            ),
            (((1,), (1,)), ((), ())),
            preferred_element_type=jnp.float32,
        )
        weights = jnp.exp2(cosine * scale)
        if k == 0 and quad == 0:
            own_row = lax.broadcasted_iota(jnp.int32, weights.shape, 0)
            own_col = lax.broadcasted_iota(jnp.int32, weights.shape, 1)
            own = (own_col < HALF) & (own_row == own_col + half * HALF)
            weights = jnp.where(own, 0.0, weights)
        start = (2 * half + quad) * 4 * HALF
        kmat[k, :, start : start + 4 * HALF] = weights.astype(jnp.bfloat16) * keep.astype(
            jnp.bfloat16
        )
        return jnp.sum(weights, axis=0, keepdims=True) * keep

    load_mask.wait()
    sums = {}
    for quad in range(2):
        keep = kept_lanes(0, quad)
        for half in range(2):
            sums[half, quad] = make_tile(uj, 0, half, quad, keep)
    whole(UNIT_PASS, ui.at[others]).wait_recv()
    keeps = [[kept_lanes(k, quad) for k in range(SIDE)] for quad in range(2)]
    for half in range(2):
        for quad in range(2):
            total = sums[half, quad]
            for k in range(1, SIDE):
                total = total + make_tile(ui, k, half, quad, keeps[quad][k])
            for j in range(4):
                degrees = total[:, j * HALF : (j + 1) * HALF]
                deg[half, 0, 4 * quad + j : 4 * quad + j + 1, :] = jnp.concatenate(
                    [degrees, degrees], axis=1
                )
        for k in FAR_FIRST:
            send(DEGREE[half], deg.at[half, 0], deg.at[half, k], gather_peer(k))
    whole(LABEL_GATHER, lab.at[others]).wait_recv()
    seeds = lab[0].astype(jnp.float32)

    def scale_half(half):
        whole(DEGREE[half], deg.at[half, others]).wait_recv()
        degree = deg[half, 0]
        for k in range(1, SIDE):
            degree = degree + pltpu.roll(deg[half, k], k, 0)
        inv_root = jnp.transpose(lax.rsqrt(degree))[:HALF]
        for k in range(SIDE):
            values = lab[k, half * HALF : (half + 1) * HALF, :].astype(jnp.float32)
            sc1[half, k] = (values * inv_root[:, k : k + 1]).astype(jnp.bfloat16)
        return inv_root[:, 0:1]

    def rows_of(half):
        return pl.ds(half * HALF, HALF)

    def product(rows, lanes, scaled):
        matrix = kmat[:, rows, lanes]
        return jnp.dot(
            matrix.reshape(-1, matrix.shape[2]),
            scaled.reshape(-1, LANES),
            preferred_element_type=jnp.float32,
        ).reshape(SIDE, -1, LANES)

    first_half, last_half = slice(0, SIDE * HALF), slice(SIDE * HALF, SIDE * CHUNK)
    own_roots = [scale_half(0)]
    acc[...] = product(slice(None), first_half, sc1[0])
    own_roots.append(scale_half(1))
    spreads = []
    for half in range(2):
        rows = rows_of(half)
        spread = acc[:, rows, :] + product(rows, last_half, sc1[1])
        spreads.append(spread[0])
        part1[:, rows, :] = spread.astype(jnp.bfloat16)
        for k in FAR_FIRST:
            send(REDUCE1[half], part1.at[k, rows, :], rcv1.at[k, rows, :], reduce_peer(SIDE - k))
    own_root = jnp.concatenate(own_roots, axis=0)
    root[...] = jnp.broadcast_to(own_root, root.shape)
    for half in range(2):
        rows = rows_of(half)
        picked = slice(half * HALF, (half + 1) * HALF)
        whole(REDUCE1[half], rcv1.at[others, rows, :]).wait_recv()
        total = spreads[half]
        for k in range(1, SIDE):
            total = total + rcv1[k, rows, :].astype(jnp.float32)
        current = MIXING * own_root[picked] * total + (1.0 - MIXING) * seeds[picked]
        sc2[half, 0] = (own_root[picked] * current).astype(jnp.bfloat16)
        for k in FAR_FIRST:
            send(GATHER2[half], sc2.at[half, 0], sc2.at[half, k], gather_peer(k))
    root_wide[...] = jnp.concatenate([root[own_rows, :]] * SIDE, axis=1)
    store_root = local(STORE_ROOT, root_wide, root_hbm)
    whole(GATHER2[0], sc2.at[0, others]).wait_recv()
    acc[...] = product(slice(None), first_half, sc2[0])
    whole(GATHER2[1], sc2.at[1, others]).wait_recv()
    for half in range(2):
        rows = rows_of(half)
        spread = acc[:, rows, :] + product(rows, last_half, sc2[1])
        part2[:, rows, :] = spread.astype(jnp.bfloat16)
        for k in FAR_FIRST:
            new_row, new_col = reduce_peer(SIDE - k)
            first = lax.div(new_col, SIDE) * SIDE
            for member in range(half * SIDE // 2, (half + 1) * SIDE // 2):
                send(
                    REDUCE2,
                    part2.at[k, member * PIECE : (member + 1) * PIECE, :],
                    parts_hbm.at[k, :, own_lanes],
                    (new_row, first + member),
                )
    for k in range(1, SIDE):
        rows = pl.ds(pl.multiple_of(swap_index(k) * PIECE, PIECE), PIECE)
        send(OWN_REDUCE2, part2.at[0, rows, :], parts_hbm.at[0, :, own_lanes], swap_peer(k))
    store_own = local(STORE_OWN, part2.at[0, own_rows, :], parts_hbm.at[0, :, own_lanes])
    store_root.wait()
    store_own.wait()
    whole(OWN_REDUCE2, rcv1.at[0, 0 : (SIDE - 1) * PIECE, :]).wait_recv()
    whole(REDUCE2, rcv1.at[others]).wait_recv()
    for copy in sent:
        copy.wait_send()


def shards(embeddings, labels, tile_mask):
    width = embeddings.shape[1]
    anywhere = pl.BlockSpec(memory_space=pl.ANY)
    units = pltpu.VMEM((SIDE, CHUNK, width), jnp.bfloat16)
    chunks = pltpu.VMEM((SIDE, CHUNK, LANES), jnp.bfloat16)
    parts, root = pl.pallas_call(
        spread_kernel,
        out_shape=(
            jax.ShapeDtypeStruct((SIDE, *labels.shape), jnp.bfloat16),
            jax.ShapeDtypeStruct(labels.shape, jnp.float32),
        ),
        in_specs=[anywhere] * 3,
        out_specs=(anywhere, anywhere),
        scratch_shapes=[
            pltpu.SMEM(tile_mask.shape, jnp.int32),
            pltpu.VMEM(embeddings.shape, jnp.bfloat16),
            units,
            units,
            pltpu.VMEM((SIDE, CHUNK, SIDE * CHUNK), jnp.bfloat16),
            chunks,
            pltpu.VMEM((2, SIDE, HALF, LANES), jnp.bfloat16),
            pltpu.VMEM((2, SIDE, HALF, LANES), jnp.bfloat16),
            chunks,
            chunks,
            chunks,
            pltpu.VMEM((SIDE, CHUNK, LANES), jnp.float32),
            pltpu.VMEM((2, SIDE, SIDE, CHUNK), jnp.float32),
            pltpu.VMEM((CHUNK, LANES), jnp.float32),
            pltpu.VMEM(labels.shape, jnp.float32),
            pltpu.SemaphoreType.DMA((PHASES,)),
            pltpu.SemaphoreType.DMA((PHASES + SLOTS,)),
            pltpu.SemaphoreType.DMA((5,)),
        ],
        compiler_params=pltpu.CompilerParams(collective_id=0, has_side_effects=True),
    )(tile_mask, embeddings, labels)
    spread = parts[0].astype(jnp.float32)
    for k in range(1, SIDE):
        spread = spread + parts[k].astype(jnp.float32)
    current = MIXING * root * spread + (1.0 - MIXING) * labels.astype(jnp.float32)
    return current.astype(jnp.bfloat16)


def solution(mesh):
    placed = (P(("row", "col"), None), P(("row", "col"), None), P())
    return jax.shard_map(
        shards, mesh=mesh, in_specs=placed, out_specs=P(("row", "col"), None), check_vma=False
    )
```
